512 devices in a mesh: slab: 32 (over y, x_lo, core), space: 16 (over x_hi, z).
Axes of the slice: x: 4 (x_hi: 2, x_lo: 2; x = x_hi * 2 + x_lo), y: 8, z: 8, core: 2. Of those that a mesh axis runs over, the one named last changes fastest.
Arguments:
- query_rows: bfloat16 [131072, 128], P(('slab', 'space')), may hold values from -4 to 4, as said below
- key_rows: bfloat16 [131072, 128], P(('slab', 'space')), may hold values from -4 to 4, as said below
- value_rows: bfloat16 [131072, 128], P(('slab', 'space')), may hold values from -6 to 6
- out_saved: bfloat16 [131072, 128], P(('slab', 'space')), may hold values from -1.796875 to 1.796875
- grad_out: bfloat16 [131072, 128], P(('slab', 'space')), may hold values from -6 to 6
- log_norm: float32 [1, 131072], P(None, ('slab', 'space')), as said below
- band_mask: int32 [6, 32, 32], replicated, may hold values from 0 to 1, as said below
- frame_of_slab: int32 [32], replicated, may hold values from 0 to 31, as said below
Outputs:
- grad_query: bfloat16 [131072, 128], P(('slab', 'space'))
- grad_key: bfloat16 [131072, 128], P(('slab', 'space'))
- grad_value: bfloat16 [131072, 128], P(('slab', 'space'))
The draws below stay inside these ranges and needn't reach their ends.
Inputs may be any that keep to these rules, and one draw needn't show every extreme that they name: query_rows are drawn afresh for each token. key_rows are drawn afresh for each token. log_norm[h, t] is the log of the sum over u with allowed[t, u] = 1 of exp(q_h(t) . k_h(u) / sqrt(128)) for the given queries and keys. band_mask[0, a, b] = 1 whenever tiles a and b differ by at most 1; band_mask[0, a, b] is 0 unless a // 2 and b // 2 differ by at most 1; for levels 1 and up, band_mask[l, a, b] is 0 unless a // 2 and b // 2 are equal. frame_of_slab names every frame once.
All inputs are finite; a program needn't handle non-finite values.
Results may differ from the reference program's by a relative error of at most 0.0075.
Values may be sent and summed in bfloat16 or wider, within the bound.
A program may use at most 64 MiB of HBM per device.

```python
import jax
import jax.numpy as jnp
from jax import lax

HEAD_DIM = 128
HEADS = 1
TILE = 128
LEVELS = 6
TOK_DEV = 256
TILES = 32
TOKENS = 131072
N_SLAB = 32
N_SPACE = 16


def frame_order(key):
    return jax.random.permutation(jax.random.fold_in(key, 11), N_SLAB).astype(jnp.int32)


def tile_pattern(key):
    per_device = TOK_DEV // TILE
    levels = jnp.arange(LEVELS, dtype=jnp.int32)
    tiles = jnp.arange(TILES, dtype=jnp.int32) // per_device
    apart = jnp.abs(tiles[:, None] - tiles[None, :])
    limits = jnp.where(levels == 0, jnp.int32(1 << 15), jnp.right_shift(jnp.int32(1 << 16), jnp.maximum(levels - 1, 0)))
    picks = jax.random.randint(jax.random.fold_in(key, 13), (LEVELS, TILES, TILES), 0, 1 << 16, dtype=jnp.int32)
    reach = jnp.where(levels[:, None, None] == 0, apart[None] <= 1, apart[None] == 0)
    chosen = reach & (picks < limits[:, None, None])
    tile_ids = jnp.arange(TILES, dtype=jnp.int32)
    near_tile = jnp.abs(tile_ids[:, None] - tile_ids[None, :]) <= 1
    diagonal = (levels[:, None, None] == 0) & near_tile[None]
    return (chosen | diagonal).astype(jnp.int32)


def token_rows(key, salt):
    shape = (TOKENS, HEADS * HEAD_DIM)
    rows = jax.random.truncated_normal(jax.random.fold_in(key, salt), -4.0, 4.0, shape, jnp.float32)
    return rows.astype(jnp.bfloat16)


def draw_query_rows(key, part):
    return token_rows(key, 21)


def draw_key_rows(key, part):
    return token_rows(key, 31)


def draw_band_mask(key, part):
    return tile_pattern(key)


def draw_frame_of_slab(key, part):
    return frame_order(key)


def draw_log_norm(key, part):
    per_device = TOK_DEV // TILE
    score_scale = HEAD_DIM ** (-0.5)
    queries = token_rows(key, 21).astype(jnp.float32).reshape(N_SLAB, N_SPACE, TOK_DEV, HEADS, HEAD_DIM)
    keys_all = token_rows(key, 31).astype(jnp.float32).reshape(N_SLAB, N_SPACE, TOK_DEV, HEADS, HEAD_DIM)
    pattern = tile_pattern(key)
    frames = frame_order(key)
    padded_mask = jnp.pad(pattern[0], ((0, 0), (per_device, per_device)))

    def window_of(column):
        start = column * per_device
        return lax.dynamic_slice(padded_mask, (start, start), (per_device, 3 * per_device))
    window_tiles = jax.vmap(window_of)(jnp.arange(N_SPACE, dtype=jnp.int32))
    window_allow = jnp.repeat(jnp.repeat(window_tiles, TILE, axis=-2), TILE, axis=-1) > 0
    padded_keys = jnp.pad(keys_all, ((0, 0), (1, 1), (0, 0), (0, 0), (0, 0)))
    wide_keys = jnp.concatenate([padded_keys[:, :-2], padded_keys[:, 1:-1], padded_keys[:, 2:]], axis=2)
    scores = jnp.einsum('spqhd,spkhd->sphqk', queries, wide_keys) * score_scale
    total = jax.nn.logsumexp(jnp.where(window_allow[None, :, None], scores, -jnp.inf), axis=-1)
    level_tiles = jnp.moveaxis(jnp.diagonal(pattern.reshape(LEVELS, N_SPACE, per_device, N_SPACE, per_device), axis1=1, axis2=3), -1, 1)
    level_allow = jnp.repeat(jnp.repeat(level_tiles, TILE, axis=-2), TILE, axis=-1) > 0
    slab_ids = jnp.arange(N_SLAB, dtype=jnp.int32)
    powers = jnp.left_shift(jnp.int32(1), jnp.arange(LEVELS - 1, dtype=jnp.int32))

    def cycle_offset(running, offset):
        source = (slab_ids - offset) % N_SLAB
        distance = jnp.abs(frames - frames[source])
        level = jnp.sum((distance[:, None] >= powers[None]).astype(jnp.int32), axis=1)
        allow = level_allow[level]
        pair_scores = jnp.einsum('spqhd,spkhd->sphqk', queries, keys_all[source]) * score_scale
        piece = jax.nn.logsumexp(jnp.where(allow[:, :, None], pair_scores, -jnp.inf), axis=-1)
        return (jnp.logaddexp(running, piece), None)
    total, unused = lax.scan(cycle_offset, total, jnp.arange(1, N_SLAB, dtype=jnp.int32))
    return total.transpose(2, 0, 1, 3).reshape(HEADS, TOKENS).astype(jnp.float32)


def steps_of(stream_key, shape, cuts, least, high):
    def one(position, shards_of):
        draws = jax.random.uniform(jax.random.fold_in(jax.random.fold_in(stream_key, 6), position), (shards_of,), jnp.float32, least / len(cuts), high / len(cuts))
        return jnp.repeat(jnp.exp(draws), shape[position] // shards_of).reshape((-1,) + (1,) * (len(shape) - position - 1))

    loudness = one(*cuts[0])
    for cut in cuts[1:]:
        loudness = loudness * one(*cut)
    return loudness


def scatter_about(own_key, dims, scale, most, cuts=(), kind=jnp.bfloat16):
    drawn = scale * jax.random.normal(own_key, dims, jnp.float32)
    if cuts:
        drawn = drawn * steps_of(own_key, dims, cuts, -0.22, 0.18)
    return jnp.clip(drawn, -most, most).astype(kind)


def setup_inputs(seed: int = 0) -> dict:
    seeds = jax.random.split(jax.random.key(seed), 9)
    return {
        "query_rows": draw_query_rows(jax.random.fold_in(seeds[8], 71), 0),
        "key_rows": draw_key_rows(jax.random.fold_in(seeds[8], 71), 0),
        "value_rows": scatter_about(seeds[2], (TOKENS, HEADS * HEAD_DIM), 1.0, 6.0, ((0, 512),)),
        "out_saved": scatter_about(seeds[3], (TOKENS, HEADS * HEAD_DIM), 0.3, 1.796875, ((0, 512),)),
        "grad_out": scatter_about(seeds[4], (TOKENS, HEADS * HEAD_DIM), 1.0, 6.0, ((0, 512),)),
        "log_norm": draw_log_norm(jax.random.fold_in(seeds[8], 71), 0),
        "band_mask": draw_band_mask(jax.random.fold_in(seeds[8], 71), 0),
        "frame_of_slab": draw_frame_of_slab(jax.random.fold_in(seeds[8], 71), 0),
    }


def expand_tiles(tile_mask, tile):
    return jnp.repeat(jnp.repeat(tile_mask, tile, axis=-2), tile, axis=-1) > 0


def level_of(distance, level_count):
    powers = jnp.left_shift(jnp.int32(1), jnp.arange(level_count - 1, dtype=jnp.int32))
    return jnp.sum((distance[..., None] >= powers).astype(jnp.int32), axis=-1)


def rounded(values_wide):
    half = values_wide.astype(jnp.bfloat16)
    return lax.optimization_barrier(half).astype(jnp.float32)


def block_grads(query, grad_rows, log_norm, delta, key_block, value_block, allow):
    head_count = log_norm.shape[0]
    query_count = query.shape[0]
    key_count = key_block.shape[0]
    head_dim = query.shape[1] // head_count
    score_scale = head_dim ** -0.5
    query_f = query.astype(jnp.float32).reshape(query_count, head_count, head_dim)
    grad_f = grad_rows.astype(jnp.float32).reshape(query_count, head_count, head_dim)
    key_f = key_block.astype(jnp.float32).reshape(key_count, head_count, head_dim)
    value_f = value_block.astype(jnp.float32).reshape(key_count, head_count, head_dim)
    scores = jnp.einsum("qhd,khd->hqk", query_f, key_f) * score_scale
    prob = jnp.where(allow[None], jnp.exp(scores - log_norm[:, :, None]), 0.0)
    dprob = jnp.einsum("qhd,khd->hqk", grad_f, value_f)
    dscore = prob * (dprob - delta[:, :, None])
    prob_half = rounded(prob)
    score_half = rounded(dscore)
    grad_query = jnp.einsum("hqk,khd->qhd", score_half, key_f).reshape(query_count, -1) * score_scale
    grad_key = jnp.einsum("hqk,qhd->khd", score_half, query_f).reshape(key_count, -1) * score_scale
    grad_value = jnp.einsum("hqk,qhd->khd", prob_half, grad_f).reshape(key_count, -1)
    return grad_query, grad_key, grad_value


def reference(query_rows, key_rows, value_rows, out_saved, grad_out, log_norm, band_mask, frame_of_slab):
    per_device = TOK_DEV // TILE
    width = HEADS * HEAD_DIM

    def blocks(rows):
        return rows.reshape(N_SLAB, N_SPACE, TOK_DEV, width)

    query_b = blocks(query_rows)
    key_b = blocks(key_rows)
    value_b = blocks(value_rows)
    grad_b = blocks(grad_out)
    stats = log_norm.reshape(HEADS, N_SLAB, N_SPACE, TOK_DEV).transpose(1, 2, 0, 3)
    product = grad_out.astype(jnp.float32) * out_saved.astype(jnp.float32)
    delta = product.reshape(N_SLAB, N_SPACE, TOK_DEV, HEADS, HEAD_DIM).sum(-1).transpose(0, 1, 3, 2)

    padded_mask = jnp.pad(band_mask[0], ((0, 0), (per_device, per_device)))
    columns = jnp.arange(N_SPACE, dtype=jnp.int32)

    def window_of(column):
        start = (column * per_device).astype(jnp.int32)
        return lax.dynamic_slice(padded_mask, (start, start), (per_device, 3 * per_device))

    window_allow = expand_tiles(jax.vmap(window_of)(columns), TILE)

    def widen(rows):
        padded = jnp.pad(rows, ((0, 0), (1, 1), (0, 0), (0, 0)))
        return jnp.concatenate([padded[:, :-2], padded[:, 1:-1], padded[:, 2:]], axis=2)

    inner = jax.vmap(block_grads, in_axes=(0, 0, 0, 0, 0, 0, 0))

    def window_slab(args):
        return inner(args[0], args[1], args[2], args[3], args[4], args[5], window_allow)

    win_q, win_k, win_v = lax.map(window_slab, (query_b, grad_b, stats, delta, widen(key_b), widen(value_b)))

    def fold_back(wide):
        own = wide[:, :, TOK_DEV:2 * TOK_DEV]
        from_lower = jnp.pad(wide[:, :, 2 * TOK_DEV:], ((0, 0), (1, 0), (0, 0), (0, 0)))[:, :-1]
        from_upper = jnp.pad(wide[:, :, :TOK_DEV], ((0, 0), (0, 1), (0, 0), (0, 0)))[:, 1:]
        return own + from_lower + from_upper

    level_tiles = jnp.moveaxis(jnp.diagonal(band_mask.reshape(LEVELS, N_SPACE, per_device, N_SPACE, per_device), axis1=1, axis2=3), -1, 1)
    level_allow = expand_tiles(level_tiles, TILE)
    slab_ids = jnp.arange(N_SLAB, dtype=jnp.int32)
    pair_grads = jax.vmap(jax.vmap(block_grads))

    def cycle_offset(sums, offset):
        grad_q, grad_k, grad_v = sums
        source = (slab_ids - offset) % N_SLAB
        level = level_of(jnp.abs(frame_of_slab - frame_of_slab[source]), LEVELS)
        part_q, part_k, part_v = pair_grads(query_b, grad_b, stats, delta, key_b[source], value_b[source], level_allow[level])
        return (grad_q + part_q, grad_k.at[source].add(part_k), grad_v.at[source].add(part_v)), None

    start = (win_q, fold_back(win_k), fold_back(win_v))
    sums, unused = lax.scan(cycle_offset, start, jnp.arange(1, N_SLAB, dtype=jnp.int32))
    grad_q, grad_k, grad_v = sums
    return (grad_q.reshape(TOKENS, width).astype(jnp.bfloat16),
            grad_k.reshape(TOKENS, width).astype(jnp.bfloat16),
            grad_v.reshape(TOKENS, width).astype(jnp.bfloat16))
```

```python
import functools
import math

import jax
import jax.numpy as jnp
from jax import lax
from jax.experimental import pallas as pl
from jax.experimental.pallas import tpu as pltpu
from jax.sharding import PartitionSpec as P

MESH = pl.DeviceIdType.MESH
TILE = 128
ROWS = 256
DIM = 128
LOG2E = math.log2(math.e)
MASKED = 1e30
BF16 = jnp.bfloat16
F32 = jnp.float32

NEXT = {1: 2, 2: 3, 3: 4, 5: 6, 6: 7}
FIRST = (1, 5)


def dot_nt(a, b):
    return lax.dot_general(a, b, (((1,), (1,)), ((), ())), preferred_element_type=F32)


def dot_nn(a, b):
    return lax.dot_general(a, b, (((1,), (0,)), ((), ())), preferred_element_type=F32)


def kernel(
    slab_count,
    space_count,
    level_count,
    q_hbm,
    k_hbm,
    v_hbm,
    o_hbm,
    g_hbm,
    lse_ref,
    band,
    frames,
    dq_hbm,
    dk_hbm,
    dv_hbm,
    qg,
    stat,
    wqg,
    wstat,
    kv,
    kt,
    o_buf,
    dk_acc,
    dv_acc,
    dq_acc,
    dq_out,
    dq_in,
    wdq_out,
    wdq_in,
    kv_out,
    kv_in,
    res,
    local_sem,
    fwd_send,
    fwd_recv,
    win_send,
    win_recv,
    kv_send,
    kv_recv,
    ret_send,
    ret_recv,
    wret_send,
    wret_recv,
    kvret_send,
    kvret_recv,
):
    m = lax.axis_index("slab")
    c = lax.axis_index("space")
    group = m % 4
    base = m - group
    core = group % 2
    x_lo = group // 2
    mate = [m, base + 2 * x_lo + (1 - core), base + 2 * (1 - x_lo) + core, base + 2 * (1 - x_lo) + (1 - core)]
    up = (m + 4) % slab_count
    down = (m + slab_count - 4) % slab_count
    left = (c + space_count - 1) % space_count
    right = (c + 1) % space_count
    scale = DIM ** (-0.5)

    loads = []

    def load(src, dst):
        copy = pltpu.make_async_copy(src, dst, local_sem.at[len(loads)])
        copy.start()
        loads.append(copy)

    for t in range(2):
        rows = pl.ds(t * TILE, TILE)
        load(q_hbm.at[rows], qg.at[0, t, 0])
        load(g_hbm.at[rows], qg.at[0, t, 1])
    load(o_hbm, o_buf)
    load(k_hbm, kv.at[0, 0])
    load(v_hbm, kv.at[0, 1])

    barrier = pltpu.get_barrier_semaphore()
    for peer in (up, down, mate[1], mate[2], mate[3]):
        pl.semaphore_signal(barrier, inc=1, device_id={"slab": peer}, device_id_type=MESH)
    for peer in (left, right):
        pl.semaphore_signal(barrier, inc=1, device_id={"space": peer}, device_id_type=MESH)

    for copy in loads:
        copy.wait()

    for t in range(2):
        product = qg[0, t, 1].astype(F32) * o_buf[pl.ds(t * TILE, TILE), :].astype(F32)
        stat[0, t, 1:2, :] = jnp.sum(product.T, axis=0, keepdims=True)
        stat[0, t, 0:1, :] = lse_ref[:, t * TILE : (t + 1) * TILE] * LOG2E

    pl.semaphore_wait(barrier, 7)

    def ring_copies(src, dst, half_from):
        out = []
        for half in range(2):
            peer = up if half == 0 else down
            s_half = half_from[half]
            for part in range(2):
                out.append(
                    pltpu.make_async_remote_copy(
                        src_ref=qg.at[src, s_half, part],
                        dst_ref=qg.at[dst, half, part],
                        send_sem=fwd_send.at[dst, half, part],
                        recv_sem=fwd_recv.at[dst, half, part],
                        device_id={"slab": peer},
                        device_id_type=MESH,
                    )
                )
            out.append(
                pltpu.make_async_remote_copy(
                    src_ref=stat.at[src, s_half],
                    dst_ref=stat.at[dst, half],
                    send_sem=fwd_send.at[dst, half, 2],
                    recv_sem=fwd_recv.at[dst, half, 2],
                    device_id={"slab": peer},
                    device_id_type=MESH,
                )
            )
        return out

    hop = {
        1: ring_copies(0, 1, (0, 1)),
        2: ring_copies(1, 2, (0, 1)),
        3: ring_copies(2, 3, (0, 1)),
        4: ring_copies(3, 4, (0, 1)),
        5: ring_copies(0, 5, (1, 0)),
        6: ring_copies(5, 6, (0, 1)),
        7: ring_copies(6, 7, (0, 1)),
    }

    def start(copies):
        for copy in copies:
            copy.start()

    def arrive(step):
        onward = hop[NEXT[step]] if step in NEXT else [None] * 6
        for n in (0, 3, 1, 4, 2, 5):
            hop[step][n].wait_recv()
            if onward[n] is not None:
                onward[n].start()

    def kv_copy(src, dst, peer, n):
        return pltpu.make_async_remote_copy(
            src_ref=kv.at[src],
            dst_ref=kv.at[dst],
            send_sem=kv_send.at[n],
            recv_sem=kv_recv.at[n],
            device_id={"slab": peer},
            device_id_type=MESH,
        )

    kv1 = kv_copy(0, 1, mate[1], 0)
    kv2 = kv_copy(0, 2, mate[2], 1)
    kv3 = kv_copy(2, 3, mate[1], 2)

    def win_copies(side, peer):
        return [
            pltpu.make_async_remote_copy(
                src_ref=qg.at[0],
                dst_ref=wqg.at[side],
                send_sem=win_send.at[side, 0],
                recv_sem=win_recv.at[side, 0],
                device_id={"space": peer},
                device_id_type=MESH,
            ),
            pltpu.make_async_remote_copy(
                src_ref=stat.at[0],
                dst_ref=wstat.at[side],
                send_sem=win_send.at[side, 1],
                recv_sem=win_recv.at[side, 1],
                device_id={"space": peer},
                device_id_type=MESH,
            ),
        ]

    win = win_copies(0, right) + win_copies(1, left)
    wret = [
        pltpu.make_async_remote_copy(
            src_ref=wdq_out.at[side],
            dst_ref=wdq_in.at[side],
            send_sem=wret_send.at[side],
            recv_sem=wret_recv.at[side],
            device_id={"space": peer},
            device_id_type=MESH,
        )
        for side, peer in ((0, left), (1, right))
    ]

    def ret_copies(step):
        return [
            pltpu.make_async_remote_copy(
                src_ref=dq_out.at[step, half],
                dst_ref=dq_in.at[step, half],
                send_sem=ret_send.at[step, half],
                recv_sem=ret_recv.at[step, half],
                device_id={"slab": down if half == 0 else up},
                device_id_type=MESH,
            )
            for half in range(2)
        ]

    ret = {step: ret_copies(step) for step in range(1, 8)}

    def kvret_copy(slot, peer):
        return pltpu.make_async_remote_copy(
            src_ref=kv_out.at[slot],
            dst_ref=kv_in.at[slot],
            send_sem=kvret_send.at[slot],
            recv_sem=kvret_recv.at[slot],
            device_id={"slab": peer},
            device_id_type=MESH,
        )

    kvret = {1: kvret_copy(1, mate[1]), 2: kvret_copy(2, mate[2]), 3: kvret_copy(3, mate[1])}

    start(hop[1])
    kv2.start()
    kv1.start()
    start(win)
    start(hop[5])

    dk_acc[...] = jnp.zeros_like(dk_acc)
    dv_acc[...] = jnp.zeros_like(dv_acc)
    kt[0] = kv[0, 0].astype(F32).T.astype(BF16)

    lane = lax.broadcasted_iota(jnp.int32, (1, ROWS), 1)

    def mask_bias(level, q_tile, k_tile):
        return jnp.where(band[level, q_tile, k_tile] > 0, 0.0, MASKED).astype(F32)

    def level_between(a, b):
        distance = jnp.abs(frames[a] - frames[b])
        level = jnp.int32(0)
        for n in range(level_count - 1):
            level = level + jnp.where(distance >= 2**n, 1, 0)
        return level

    def pair(q, g, lse, delta, biases, j):
        key = kv[j, 0]
        shift = [lse + jnp.where(lane < TILE, biases[t][0], biases[t][1]) for t in range(2)]
        shifts = jnp.concatenate(
            [jnp.broadcast_to(shift[t], (TILE, ROWS)) for t in range(2)], axis=0
        )
        prob = jnp.exp2(dot_nt(key, q) * (scale * LOG2E) - shifts)
        dprob = dot_nt(kv[j, 1], g)
        dscore = (prob * (dprob - delta)).astype(BF16)
        dv_acc[j] += dot_nn(prob.astype(BF16), g)
        dk_acc[j] += dot_nn(dscore, q)
        return dot_nn(kt[j], dscore)

    def step_compute(s):
        hops = jnp.where(s <= 4, s, s - 4)
        first = jnp.where(s <= 4, 0, 1)
        source = [
            (m + slab_count - 4 * hops) % slab_count,
            (m + 4 * hops) % slab_count,
        ]
        q_tile = [2 * c + first, 2 * c + (1 - first)]
        block = [jnp.concatenate([qg[s, 0, n], qg[s, 1, n]], axis=0) for n in range(2)]
        lse = jnp.concatenate([stat[s, 0, 0:1, :], stat[s, 1, 0:1, :]], axis=1)
        delta = jnp.concatenate([stat[s, 0, 1:2, :], stat[s, 1, 1:2, :]], axis=1)
        total = jnp.zeros((DIM, ROWS), F32)
        for j in range(4):
            level = [level_between(source[half], mate[j]) for half in range(2)]
            biases = [
                [mask_bias(level[half], q_tile[half], 2 * c + t) for half in range(2)]
                for t in range(2)
            ]
            total = total + pair(block[0], block[1], lse, delta, biases, j)
        dq_acc[s] = total

    def window_compute(side):
        away = c - 1 if side == 0 else c + 1
        there = left if side == 0 else right
        inside = jnp.where((away >= 0) & (away < space_count), 1, 0)
        block = [
            jnp.concatenate([wqg[side, 0, n], wqg[side, 1, n]], axis=0) for n in range(2)
        ]
        lse = jnp.concatenate([wstat[side, 0, 0:1, :], wstat[side, 1, 0:1, :]], axis=1)
        delta = jnp.concatenate([wstat[side, 0, 1:2, :], wstat[side, 1, 1:2, :]], axis=1)
        biases = [
            [
                jnp.where(band[0, 2 * there + half, 2 * c + t] * inside > 0, 0.0, MASKED).astype(F32)
                for half in range(2)
            ]
            for t in range(2)
        ]
        part = pair(block[0], block[1], lse, delta, biases, 0)
        for half in range(2):
            wdq_out[side, half] = part[:, half * TILE : (half + 1) * TILE].astype(BF16)

    def send_back(step, prior):
        for half in range(2):
            part = dq_acc[step, :, half * TILE : (half + 1) * TILE]
            if prior is not None:
                ret[prior][half].wait_recv()
                part = part + dq_in[prior, half].astype(F32)
            dq_out[step, half] = part.astype(BF16)
            ret[step][half].start()

    arrive(1)
    kv2.wait_recv()
    kv3.start()
    for copy in win:
        copy.wait_recv()
    for side in range(2):
        window_compute(side)
        wret[side].start()
    kv1.wait_recv()
    kt[1] = kv[1, 0].astype(F32).T.astype(BF16)
    kt[2] = kv[2, 0].astype(F32).T.astype(BF16)
    kv3.wait_recv()
    kt[3] = kv[3, 0].astype(F32).T.astype(BF16)

    def turn(s, carry):
        for n in range(1, 7):
            @pl.when(s == n - 1)
            def _():
                arrive(n + 1)

        step_compute(s)

        @pl.when(s == 4)
        def _():
            send_back(4, None)

        @pl.when(s == 5)
        def _():
            send_back(3, 4)

        @pl.when(s == 6)
        def _():
            send_back(2, 3)

        return carry

    lax.fori_loop(0, 8, turn, 0)

    def pack(j, extra=None):
        dk = dk_acc[j]
        dv = dv_acc[j]
        if extra is not None:
            dk = dk + kv_in[extra, 0].astype(F32)
            dv = dv + kv_in[extra, 1].astype(F32)
        kv_out[j, 0] = dk.astype(BF16)
        kv_out[j, 1] = dv.astype(BF16)

    pack(3)
    kvret[3].start()
    send_back(7, None)
    pack(1)
    kvret[1].start()
    send_back(1, 2)
    kvret[3].wait_recv()
    pack(2, 3)
    kvret[2].start()
    send_back(6, 7)
    send_back(5, 6)

    for side in range(2):
        wret[side].wait_recv()
    total = [dq_acc[0, :, half * TILE : (half + 1) * TILE] for half in range(2)]
    for half in range(2):
        for side in range(2):
            total[half] = total[half] + wdq_in[side, half].astype(F32)
        ret[1][half].wait_recv()
        total[half] = total[half] + dq_in[1, half].astype(F32)
    for half in range(2):
        ret[5][half].wait_recv()
        total[1 - half] = total[1 - half] + dq_in[5, half].astype(F32)
    for half in range(2):
        res[0, half * TILE : (half + 1) * TILE, :] = (total[half].T * scale).astype(BF16)
    stores = [pltpu.make_async_copy(res.at[0], dq_hbm, local_sem.at[0])]
    stores[0].start()

    for slot in (1, 2):
        kvret[slot].wait_recv()
    dk = dk_acc[0] + kv_in[1, 0].astype(F32) + kv_in[2, 0].astype(F32)
    dv = dv_acc[0] + kv_in[1, 1].astype(F32) + kv_in[2, 1].astype(F32)
    res[1] = (dk * scale).astype(BF16)
    res[2] = dv.astype(BF16)
    for n, out in ((1, dk_hbm), (2, dv_hbm)):
        copy = pltpu.make_async_copy(res.at[n], out, local_sem.at[n])
        copy.start()
        stores.append(copy)

    for step in range(1, 8):
        for copy in hop[step]:
            copy.wait_send()
        for copy in ret[step]:
            copy.wait_send()
    for copy in win + wret + [kv1, kv2, kv3] + list(kvret.values()) + []:
        copy.wait_send()
    for copy in stores:
        copy.wait()


def body(slab_count, space_count, query, key, value, out_saved, grad_out, log_norm, band, frames):
    any_spec = pl.BlockSpec(memory_space=pl.ANY)
    smem = pl.BlockSpec(memory_space=pltpu.SMEM)
    vmem = pl.BlockSpec(memory_space=pltpu.VMEM)
    rows = jax.ShapeDtypeStruct((ROWS, DIM), BF16)
    dma = pltpu.SemaphoreType.DMA
    return pl.pallas_call(
        functools.partial(kernel, slab_count, space_count, band.shape[0]),
        out_shape=(rows, rows, rows),
        in_specs=[any_spec] * 5 + [vmem, smem, smem],
        out_specs=[any_spec] * 3,
        scratch_shapes=[
            pltpu.VMEM((8, 2, 2, TILE, DIM), BF16),
            pltpu.VMEM((8, 2, 2, TILE), F32),
            pltpu.VMEM((2, 2, 2, TILE, DIM), BF16),
            pltpu.VMEM((2, 2, 2, TILE), F32),
            pltpu.VMEM((4, 2, ROWS, DIM), BF16),
            pltpu.VMEM((4, DIM, ROWS), BF16),
            pltpu.VMEM((ROWS, DIM), BF16),
            pltpu.VMEM((4, ROWS, DIM), F32),
            pltpu.VMEM((4, ROWS, DIM), F32),
            pltpu.VMEM((8, DIM, ROWS), F32),
            pltpu.VMEM((8, 2, DIM, TILE), BF16),
            pltpu.VMEM((8, 2, DIM, TILE), BF16),
            pltpu.VMEM((2, 2, DIM, TILE), BF16),
            pltpu.VMEM((2, 2, DIM, TILE), BF16),
            pltpu.VMEM((4, 2, ROWS, DIM), BF16),
            pltpu.VMEM((4, 2, ROWS, DIM), BF16),
            pltpu.VMEM((3, ROWS, DIM), BF16),
            dma((8,)),
            dma((8, 2, 3)),
            dma((8, 2, 3)),
            dma((2, 2)),
            dma((2, 2)),
            dma((3,)),
            dma((3,)),
            dma((8, 2)),
            dma((8, 2)),
            dma((2,)),
            dma((2,)),
            dma((4,)),
            dma((4,)),
        ],
        compiler_params=pltpu.CompilerParams(
            collective_id=0, has_side_effects=True, vmem_limit_bytes=32 * 1024 * 1024
        ),
    )(query, key, value, out_saved, grad_out, log_norm, band, frames)


def solution(mesh):
    rows = P(("slab", "space"), None)
    return jax.shard_map(
        functools.partial(body, mesh.shape["slab"], mesh.shape["space"]),
        mesh=mesh,
        in_specs=(rows, rows, rows, rows, rows, P(None, ("slab", "space")), P(), P()),
        out_specs=(rows, rows, rows),
        check_vma=False,
    )
```

```python
import functools
import math

import jax
import jax.numpy as jnp
from jax import lax
from jax.experimental import pallas as pl
from jax.experimental.pallas import tpu as pltpu
from jax.sharding import PartitionSpec as P

MESH = pl.DeviceIdType.MESH
TILE = 128
ROWS = 256
DIM = 128
LOG2E = math.log2(math.e)
MASKED = 1e30
BF16 = jnp.bfloat16
F32 = jnp.float32

ONWARD = {1: 3, 2: 4, 3: 5, 4: 6}
STEPS = 8


def dot_nt(a, b):
    return lax.dot_general(a, b, (((1,), (1,)), ((), ())), preferred_element_type=F32)


def dot_nn(a, b):
    return lax.dot_general(a, b, (((1,), (0,)), ((), ())), preferred_element_type=F32)


def kernel(
    slab_count,
    space_count,
    level_count,
    q_hbm,
    k_hbm,
    v_hbm,
    o_hbm,
    g_hbm,
    lse_ref,
    band,
    frames,
    dq_hbm,
    dk_hbm,
    dv_hbm,
    qg,
    stat,
    wqg,
    wstat,
    kv,
    kt,
    o_buf,
    dk_acc,
    dv_acc,
    dq_acc,
    dq_out,
    dq_in,
    wdq_out,
    wdq_in,
    kv_out,
    kv_in,
    res,
    local_sem,
    fwd_send,
    fwd_recv,
    win_send,
    win_recv,
    kv_send,
    kv_recv,
    ret_send,
    ret_recv,
    wret_send,
    wret_recv,
    kvret_send,
    kvret_recv,
):
    m = lax.axis_index("slab")
    c = lax.axis_index("space")
    group = m % 4
    base = m - group
    core = group % 2
    x_lo = group // 2
    mate = [m, base + 2 * x_lo + (1 - core), base + 2 * (1 - x_lo) + core, base + 2 * (1 - x_lo) + (1 - core)]
    up = (m + 4) % slab_count
    down = (m + slab_count - 4) % slab_count
    left = (c + space_count - 1) % space_count
    right = (c + 1) % space_count
    scale = DIM ** (-0.5)

    loads = []

    def load(src, dst):
        copy = pltpu.make_async_copy(src, dst, local_sem.at[len(loads)])
        copy.start()
        loads.append(copy)

    for t in range(2):
        rows = pl.ds(t * TILE, TILE)
        load(q_hbm.at[rows], qg.at[0, t, 0])
        load(g_hbm.at[rows], qg.at[0, t, 1])
    load(o_hbm, o_buf)
    load(k_hbm, kv.at[0, 0])
    load(v_hbm, kv.at[0, 1])

    def ring(hops):
        return (m + 4 * hops + slab_count) % slab_count

    barrier = pltpu.get_barrier_semaphore()
    peers = [ring(hops) for hops in (-3, -2, -1, 1, 2, 3, 4)] + mate[1:]
    for peer in peers:
        pl.semaphore_signal(barrier, inc=1, device_id={"slab": peer}, device_id_type=MESH)
    for peer in (left, right):
        pl.semaphore_signal(barrier, inc=1, device_id={"space": peer}, device_id_type=MESH)

    for copy in loads:
        copy.wait()

    for t in range(2):
        product = qg[0, t, 1].astype(F32) * o_buf[pl.ds(t * TILE, TILE), :].astype(F32)
        stat[0, t, 1:2, :] = jnp.sum(product.T, axis=0, keepdims=True)
        stat[0, t, 0:1, :] = lse_ref[:, t * TILE : (t + 1) * TILE] * LOG2E

    pl.semaphore_wait(barrier, len(peers) + 2)

    def frame_copies(src, dst, peer, tiles=(0, 1)):
        out = {}
        for tile in tiles:
            for part in range(3):
                big = part < 2
                out[tile, part] = pltpu.make_async_remote_copy(
                    src_ref=qg.at[src, tile, part] if big else stat.at[src, tile],
                    dst_ref=qg.at[dst, tile, part] if big else stat.at[dst, tile],
                    send_sem=fwd_send.at[dst, tile, part],
                    recv_sem=fwd_recv.at[dst, tile, part],
                    device_id={"slab": peer},
                    device_id_type=MESH,
                )
        return out

    hop = {}
    for s in range(1, 7):
        hop[s] = frame_copies(max(s - 2, 0), s, up if s % 2 else down)
    far = {0: frame_copies(3, 7, ring(2), (0,)), 1: frame_copies(4, 7, ring(-2), (1,))}
    hop[7] = {**far[0], **far[1]}

    def start(copies):
        for copy in copies.values():
            copy.start()

    def arrive(step):
        for key, copy in hop[step].items():
            copy.wait_recv()
            if step in (3, 4) and key[0] == step - 3:
                hop[7][key].start()
            if step in ONWARD:
                hop[ONWARD[step]][key].start()

    def kv_copy(src, dst, peer, n):
        return pltpu.make_async_remote_copy(
            src_ref=kv.at[src],
            dst_ref=kv.at[dst],
            send_sem=kv_send.at[n],
            recv_sem=kv_recv.at[n],
            device_id={"slab": peer},
            device_id_type=MESH,
        )

    kv1 = kv_copy(0, 1, mate[1], 0)
    kv2 = kv_copy(0, 2, mate[2], 1)
    kv3 = kv_copy(2, 3, mate[1], 2)

    def win_copies(side, peer):
        return [
            pltpu.make_async_remote_copy(
                src_ref=qg.at[0],
                dst_ref=wqg.at[side],
                send_sem=win_send.at[side, 0],
                recv_sem=win_recv.at[side, 0],
                device_id={"space": peer},
                device_id_type=MESH,
            ),
            pltpu.make_async_remote_copy(
                src_ref=stat.at[0],
                dst_ref=wstat.at[side],
                send_sem=win_send.at[side, 1],
                recv_sem=win_recv.at[side, 1],
                device_id={"space": peer},
                device_id_type=MESH,
            ),
        ]

    win = win_copies(0, right) + win_copies(1, left)
    wret = [
        pltpu.make_async_remote_copy(
            src_ref=wdq_out.at[side],
            dst_ref=wdq_in.at[side],
            send_sem=wret_send.at[side],
            recv_sem=wret_recv.at[side],
            device_id={"space": peer},
            device_id_type=MESH,
        )
        for side, peer in ((0, left), (1, right))
    ]

    def source(step):
        return ring(jnp.where(step % 2 == 1, -1, 1) * ((step + 1) // 2))

    def ret(step):
        return pltpu.make_async_remote_copy(
            src_ref=dq_out.at[step],
            dst_ref=dq_in.at[step],
            send_sem=ret_send.at[step],
            recv_sem=ret_recv.at[step],
            device_id={"slab": source(step)},
            device_id_type=MESH,
        )

    def kvret_copy(slot, peer):
        return pltpu.make_async_remote_copy(
            src_ref=kv_out.at[slot],
            dst_ref=kv_in.at[slot],
            send_sem=kvret_send.at[slot],
            recv_sem=kvret_recv.at[slot],
            device_id={"slab": peer},
            device_id_type=MESH,
        )

    kvret = {1: kvret_copy(1, mate[1]), 2: kvret_copy(2, mate[2]), 3: kvret_copy(3, mate[1])}

    start(hop[1])
    start(hop[2])
    kv2.start()
    kv1.start()
    for copy in win:
        copy.start()

    dk_acc[...] = jnp.zeros_like(dk_acc)
    dv_acc[...] = jnp.zeros_like(dv_acc)
    kt[0] = kv[0, 0].astype(F32).T.astype(BF16)

    lane = lax.broadcasted_iota(jnp.int32, (1, ROWS), 1)

    def mask_bias(level, q_tile, k_tile):
        return jnp.where(band[level, q_tile, k_tile] > 0, 0.0, MASKED).astype(F32)

    def level_between(a, b):
        distance = jnp.abs(frames[a] - frames[b])
        level = jnp.int32(0)
        for n in range(level_count - 1):
            level = level + jnp.where(distance >= 2**n, 1, 0)
        return level

    def pair(q, g, lse, delta, biases, j):
        key = kv[j, 0]
        shift = [lse + jnp.where(lane < TILE, biases[t][0], biases[t][1]) for t in range(2)]
        shifts = jnp.concatenate(
            [jnp.broadcast_to(shift[t], (TILE, ROWS)) for t in range(2)], axis=0
        )
        prob = jnp.exp2(dot_nt(key, q) * (scale * LOG2E) - shifts)
        dprob = dot_nt(kv[j, 1], g)
        dscore = (prob * (dprob - delta)).astype(BF16)
        dv_acc[j] += dot_nn(prob.astype(BF16), g)
        dk_acc[j] += dot_nn(dscore, q)
        return dot_nn(kt[j], dscore)

    def frame(s):
        block = [jnp.concatenate([qg[s, 0, n], qg[s, 1, n]], axis=0) for n in range(2)]
        row = [
            jnp.concatenate([stat[s, 0, n : n + 1, :], stat[s, 1, n : n + 1, :]], axis=1)
            for n in range(2)
        ]
        return block + row

    def visit(s, j):
        level = level_between(source(s) if not isinstance(s, int) else m, mate[j])
        biases = [[mask_bias(level, 2 * c + h, 2 * c + t) for h in range(2)] for t in range(2)]
        return pair(*frame(s), biases, j)

    def window_compute(side):
        away = c - 1 if side == 0 else c + 1
        there = left if side == 0 else right
        inside = jnp.where((away >= 0) & (away < space_count), 1, 0)
        block = [
            jnp.concatenate([wqg[side, 0, n], wqg[side, 1, n]], axis=0) for n in range(2)
        ]
        lse = jnp.concatenate([wstat[side, 0, 0:1, :], wstat[side, 1, 0:1, :]], axis=1)
        delta = jnp.concatenate([wstat[side, 0, 1:2, :], wstat[side, 1, 1:2, :]], axis=1)
        biases = [
            [
                jnp.where(band[0, 2 * there + half, 2 * c + t] * inside > 0, 0.0, MASKED).astype(F32)
                for half in range(2)
            ]
            for t in range(2)
        ]
        part = pair(block[0], block[1], lse, delta, biases, 0)
        wdq_out[side] = part.astype(BF16)

    def key_t(j):
        kt[j] = kv[j, 0].astype(F32).T.astype(BF16)

    dq_acc[...] = visit(0, 0)
    kv1.wait_recv()
    key_t(1)
    dq_acc[...] += visit(0, 1)
    arrive(1)
    arrive(2)
    kv2.wait_recv()
    kv3.start()
    key_t(2)
    dq_acc[...] += visit(0, 2)
    for copy in win:
        copy.wait_recv()
    for side in range(2):
        window_compute(side)
        wret[side].start()
    kv3.wait_recv()
    key_t(3)
    dq_acc[...] += visit(0, 3)

    def turn(s, carry):
        for n in range(1, 6):
            @pl.when(s == n)
            def _():
                arrive(n + 2)

        total = visit(s, 0)
        for j in range(1, 4):
            total = total + visit(s, j)
        dq_out[s] = total.astype(BF16)
        ret(s).start()
        return carry

    lax.fori_loop(1, STEPS, turn, 0)

    def pack(j, extra=None):
        dk = dk_acc[j]
        dv = dv_acc[j]
        if extra is not None:
            dk = dk + kv_in[extra, 0].astype(F32)
            dv = dv + kv_in[extra, 1].astype(F32)
        kv_out[j, 0] = dk.astype(BF16)
        kv_out[j, 1] = dv.astype(BF16)

    pack(3)
    kvret[3].start()
    pack(1)
    kvret[1].start()
    kvret[3].wait_recv()
    pack(2, 3)
    kvret[2].start()

    total = dq_acc[...]
    for side in range(2):
        wret[side].wait_recv()
        total = total + wdq_in[side].astype(F32)
    for step in range(1, STEPS):
        ret(jnp.int32(step)).wait_recv()
        total = total + dq_in[step].astype(F32)
    res[0] = (total.T * scale).astype(BF16)
    stores = [pltpu.make_async_copy(res.at[0], dq_hbm, local_sem.at[0])]
    stores[0].start()

    for slot in (1, 2):
        kvret[slot].wait_recv()
    dk = dk_acc[0] + kv_in[1, 0].astype(F32) + kv_in[2, 0].astype(F32)
    dv = dv_acc[0] + kv_in[1, 1].astype(F32) + kv_in[2, 1].astype(F32)
    res[1] = (dk * scale).astype(BF16)
    res[2] = dv.astype(BF16)
    for n, out in ((1, dk_hbm), (2, dv_hbm)):
        copy = pltpu.make_async_copy(res.at[n], out, local_sem.at[n])
        copy.start()
        stores.append(copy)

    for step in range(1, STEPS):
        for copy in hop[step].values():
            copy.wait_send()
        ret(jnp.int32(step)).wait_send()
    for copy in win + wret + [kv1, kv2, kv3] + list(kvret.values()):
        copy.wait_send()
    for copy in stores:
        copy.wait()


def body(slab_count, space_count, query, key, value, out_saved, grad_out, log_norm, band, frames):
    any_spec = pl.BlockSpec(memory_space=pl.ANY)
    smem = pl.BlockSpec(memory_space=pltpu.SMEM)
    vmem = pl.BlockSpec(memory_space=pltpu.VMEM)
    rows = jax.ShapeDtypeStruct((ROWS, DIM), BF16)
    dma = pltpu.SemaphoreType.DMA
    return pl.pallas_call(
        functools.partial(kernel, slab_count, space_count, band.shape[0]),
        out_shape=(rows, rows, rows),
        in_specs=[any_spec] * 5 + [vmem, smem, smem],
        out_specs=[any_spec] * 3,
        scratch_shapes=[
            pltpu.VMEM((8, 2, 2, TILE, DIM), BF16),
            pltpu.VMEM((8, 2, 2, TILE), F32),
            pltpu.VMEM((2, 2, 2, TILE, DIM), BF16),
            pltpu.VMEM((2, 2, 2, TILE), F32),
            pltpu.VMEM((4, 2, ROWS, DIM), BF16),
            pltpu.VMEM((4, DIM, ROWS), BF16),
            pltpu.VMEM((ROWS, DIM), BF16),
            pltpu.VMEM((4, ROWS, DIM), F32),
            pltpu.VMEM((4, ROWS, DIM), F32),
            pltpu.VMEM((DIM, ROWS), F32),
            pltpu.VMEM((8, DIM, ROWS), BF16),
            pltpu.VMEM((8, DIM, ROWS), BF16),
            pltpu.VMEM((2, DIM, ROWS), BF16),
            pltpu.VMEM((2, DIM, ROWS), BF16),
            pltpu.VMEM((4, 2, ROWS, DIM), BF16),
            pltpu.VMEM((4, 2, ROWS, DIM), BF16),
            pltpu.VMEM((3, ROWS, DIM), BF16),
            dma((8,)),
            dma((8, 2, 3)),
            dma((8, 2, 3)),
            dma((2, 2)),
            dma((2, 2)),
            dma((3,)),
            dma((3,)),
            dma((8,)),
            dma((8,)),
            dma((2,)),
            dma((2,)),
            dma((4,)),
            dma((4,)),
        ],
        compiler_params=pltpu.CompilerParams(
            collective_id=0, has_side_effects=True, vmem_limit_bytes=63 * 1024 * 1024
        ),
    )(query, key, value, out_saved, grad_out, log_norm, band, frames)


def solution(mesh):
    rows = P(("slab", "space"), None)
    return jax.shard_map(
        functools.partial(body, mesh.shape["slab"], mesh.shape["space"]),
        mesh=mesh,
        in_specs=(rows, rows, rows, rows, rows, P(None, ("slab", "space")), P(), P()),
        out_specs=(rows, rows, rows),
        check_vma=False,
    )
```

```python
import functools
import math

import jax
import jax.numpy as jnp
from jax import lax
from jax.experimental import pallas as pl
from jax.experimental.pallas import tpu as pltpu
from jax.sharding import PartitionSpec as P

MESH = pl.DeviceIdType.MESH
TILE = 128
ROWS = 256
DIM = 128
LOG2E = math.log2(math.e)
MASKED = 1e30
BF16 = jnp.bfloat16
F32 = jnp.float32

ONWARD = {1: 3, 2: 4, 3: 5, 4: 6}
STEPS = 8


def dot_nt(a, b):
    return lax.dot_general(a, b, (((1,), (1,)), ((), ())), preferred_element_type=F32)


def dot_nn(a, b):
    return lax.dot_general(a, b, (((1,), (0,)), ((), ())), preferred_element_type=F32)


def kernel(
    slab_count,
    space_count,
    level_count,
    q_hbm,
    k_hbm,
    v_hbm,
    o_hbm,
    g_hbm,
    lse_ref,
    band,
    frames,
    dq_hbm,
    dk_hbm,
    dv_hbm,
    qg,
    stat,
    wqg,
    wstat,
    kv,
    kt,
    o_buf,
    dk_acc,
    dv_acc,
    dq_acc,
    dq_out,
    dq_in,
    wdq_out,
    wdq_in,
    kv_out,
    kv_in,
    res,
    local_sem,
    fwd_send,
    fwd_recv,
    win_send,
    win_recv,
    kv_send,
    kv_recv,
    ret_send,
    ret_recv,
    wret_send,
    wret_recv,
    kvret_send,
    kvret_recv,
):
    m = lax.axis_index("slab")
    c = lax.axis_index("space")
    group = m % 4
    base = m - group
    core = group % 2
    x_lo = group // 2
    mate = [
        m,
        base + 2 * x_lo + (1 - core),
        base + 2 * (1 - x_lo) + core,
        base + 2 * (1 - x_lo) + (1 - core),
    ]
    scale = DIM ** (-0.5)
    has = [c > 0, c < space_count - 1]
    beside = [jnp.maximum(c - 1, 0), jnp.minimum(c + 1, space_count - 1)]
    odd = c % 2 == 1

    def ring(hops):
        return (m + 4 * hops + slab_count) % slab_count

    up, down = ring(1), ring(-1)

    barrier = pltpu.get_barrier_semaphore()
    for peer in (up, down, mate[2], mate[1]):
        pl.semaphore_signal(barrier, inc=1, device_id={"slab": peer}, device_id_type=MESH)
    for side in range(2):
        @pl.when(has[side] & jnp.logical_not(odd))
        def _():
            pl.semaphore_signal(
                barrier, inc=1, device_id={"space": beside[side]}, device_id_type=MESH
            )

    loads = [
        pltpu.make_async_copy(src, dst, local_sem.at[n])
        for n, (src, dst) in enumerate(
            (
                (g_hbm, qg.at[0, 1]),
                (o_hbm, o_buf),
                (k_hbm, kv.at[0, 0]),
                (q_hbm, qg.at[0, 0]),
                (v_hbm, kv.at[0, 1]),
            )
        )
    ]
    for copy in loads:
        copy.start()

    def remote(src, dst, sems, index, peer):
        return pltpu.make_async_remote_copy(
            src_ref=src,
            dst_ref=dst,
            send_sem=sems[0].at[index],
            recv_sem=sems[1].at[index],
            device_id=peer,
            device_id_type=MESH,
        )

    fwd, kvs, wins = (fwd_send, fwd_recv), (kv_send, kv_recv), (win_send, win_recv)
    own = (q_hbm, g_hbm)

    def frame_copies(src, dst, peer, tiles=(0, 1)):
        out = {}
        for tile in tiles:
            rows = pl.ds(tile * TILE, TILE)
            for part in range(2):
                source_ref = own[part].at[rows] if src == 0 else qg.at[src, part, rows]
                out[tile, part] = remote(
                    source_ref, qg.at[dst, part, rows], fwd, (dst, tile, part), {"slab": peer}
                )
            out[tile, 2] = remote(
                stat.at[src, tile], stat.at[dst, tile], fwd, (dst, tile, 2), {"slab": peer}
            )
        return out

    hop = {}
    for s in range(1, 7):
        hop[s] = frame_copies(max(s - 2, 0), s, up if s % 2 else down)
    far = {0: frame_copies(3, 7, ring(2), (0,)), 1: frame_copies(4, 7, ring(-2), (1,))}
    hop[7] = {**far[0], **far[1]}

    def arrive(step):
        for key, copy in hop[step].items():
            copy.wait_recv()
            if step in ONWARD:
                hop[ONWARD[step]][key].start()
        if step == 4:
            for copy in hop[7].values():
                copy.start()

    kv1 = [remote(h, kv.at[1, n], kvs, n, {"slab": mate[1]}) for n, h in enumerate((k_hbm, v_hbm))]
    kv2 = [
        remote(h, kv.at[2, n], kvs, 2 + n, {"slab": mate[2]}) for n, h in enumerate((k_hbm, v_hbm))
    ]
    kv3 = remote(kv.at[2], kv.at[3], kvs, 4, {"slab": mate[1]})

    win = [
        [
            remote(q_hbm, wqg.at[side, 0], wins, (side, 0), {"space": beside[1 - side]}),
            remote(g_hbm, wqg.at[side, 1], wins, (side, 1), {"space": beside[1 - side]}),
            remote(stat.at[0], wstat.at[side], wins, (side, 2), {"space": beside[1 - side]}),
        ]
        for side in range(2)
    ]
    wret = [
        remote(
            wdq_out.at[side], wdq_in.at[side], (wret_send, wret_recv), side, {"space": beside[side]}
        )
        for side in range(2)
    ]

    def source(step):
        return ring(jnp.where(step % 2 == 1, -1, 1) * ((step + 1) // 2))

    def ret(step):
        return remote(
            dq_out.at[step], dq_in.at[step], (ret_send, ret_recv), step, {"slab": source(step)}
        )

    kvret = {
        slot: remote(
            kv_out.at[slot], kv_in.at[slot], (kvret_send, kvret_recv), slot, {"slab": mate[peer]}
        )
        for slot, peer in ((1, 1), (2, 2), (3, 1))
    }

    pl.semaphore_wait(
        barrier, 4 + jnp.where(odd, has[0].astype(jnp.int32) + has[1].astype(jnp.int32), 0)
    )

    for key in ((0, 0), (0, 1), (1, 0), (1, 1)):
        hop[1][key].start()
        hop[2][key].start()
    for copy in kv2 + kv1:
        copy.start()

    for copy in loads[:2]:
        copy.wait()
    for t in range(2):
        rows = pl.ds(t * TILE, TILE)
        product = qg[0, 1, rows, :].astype(F32) * o_buf[rows, :].astype(F32)
        stat[0, t, 1:2, :] = jnp.sum(product.T, axis=0, keepdims=True)
        stat[0, t, 0:1, :] = lse_ref[:, t * TILE : (t + 1) * TILE] * LOG2E
    for tile in range(2):
        hop[1][tile, 2].start()
        hop[2][tile, 2].start()

    def win_start(side):
        for copy in win[side]:
            copy.start()

    for side in range(2):
        @pl.when(odd & has[1 - side])
        def _():
            win_start(side)

    for copy in loads[2:]:
        copy.wait()

    lane = lax.broadcasted_iota(jnp.int32, (1, ROWS), 1)

    def mask_bias(level, q_tile, k_tile):
        return jnp.where(band[level, q_tile, k_tile] > 0, 0.0, MASKED).astype(F32)

    def level_between(a, b):
        distance = jnp.abs(frames[a] - frames[b])
        level = jnp.int32(0)
        for n in range(level_count - 1):
            level = level + jnp.where(distance >= 2**n, 1, 0)
        return level

    def key_t(j):
        kt[j] = kv[j, 0].astype(F32).T.astype(BF16)

    def pair(q, g, lse, delta, biases, j, fresh=False):
        key = kv[j, 0]
        shift = [lse + jnp.where(lane < TILE, biases[t][0], biases[t][1]) for t in range(2)]
        shifts = jnp.concatenate(
            [jnp.broadcast_to(shift[t], (TILE, ROWS)) for t in range(2)], axis=0
        )
        prob = jnp.exp2(dot_nt(key, q) * (scale * LOG2E) - shifts)
        dprob = dot_nt(kv[j, 1], g)
        dscore = (prob * (dprob - delta)).astype(BF16)
        dv = dot_nn(prob.astype(BF16), g)
        dk = dot_nn(dscore, q)
        dv_acc[j] = dv if fresh else dv_acc[j] + dv
        dk_acc[j] = dk if fresh else dk_acc[j] + dk
        return dot_nn(kt[j], dscore)

    def frame(block, rows, s):
        return [block[s, 0], block[s, 1]] + [
            jnp.concatenate([rows[s, 0, n : n + 1, :], rows[s, 1, n : n + 1, :]], axis=1)
            for n in range(2)
        ]

    def visit(s, j, fresh=False):
        level = level_between(source(s), mate[j]) if not fresh else level_between(m, mate[j])
        biases = [[mask_bias(level, 2 * c + h, 2 * c + t) for h in range(2)] for t in range(2)]
        return pair(*frame(qg, stat, s), biases, j, fresh)

    key_t(0)
    dq_acc[...] = visit(0, 0, True)
    for copy in kv1:
        copy.wait_recv()
    key_t(1)
    dq_acc[...] += visit(0, 1, True)
    arrive(1)
    arrive(2)
    for copy in kv2:
        copy.wait_recv()
    kv3.start()
    key_t(2)
    dq_acc[...] += visit(0, 2, True)
    kv3.wait_recv()
    key_t(3)
    dq_acc[...] += visit(0, 3, True)

    def turn(s, carry):
        for n in range(1, 6):
            @pl.when(s == n)
            def _():
                arrive(n + 2)

        @pl.when(s == 4)
        def _():
            for side in range(2):
                @pl.when(has[side] & jnp.logical_not(odd))
                def _():
                    for copy in win[side]:
                        copy.wait_recv()
                    win_start(1 - side)

        total = visit(s, 0)
        for j in range(1, 4):
            total = total + visit(s, j)
        dq_out[s] = total.astype(BF16)
        ret(s).start()
        return carry

    lax.fori_loop(1, STEPS - 1, turn, 0)

    def pack(j, extra=None):
        dk = dk_acc[j]
        dv = dv_acc[j]
        if extra is not None:
            dk = dk + kv_in[extra, 0].astype(F32)
            dv = dv + kv_in[extra, 1].astype(F32)
        kv_out[j, 0] = dk.astype(BF16)
        kv_out[j, 1] = dv.astype(BF16)

    last = jnp.int32(STEPS - 1)
    total = visit(last, 3)
    pack(3)
    kvret[3].start()
    for j in (2, 1, 0):
        total = total + visit(last, j)
    dq_out[last] = total.astype(BF16)
    ret(last).start()
    pack(1)
    kvret[1].start()
    kvret[3].wait_recv()
    pack(2, 3)
    kvret[2].start()

    for side in range(2):
        @pl.when(has[side])
        def _():
            @pl.when(odd)
            def _():
                for copy in win[side]:
                    copy.wait_recv()
            biases = [
                [mask_bias(0, 2 * beside[side] + h, 2 * c + t) for h in range(2)] for t in range(2)
            ]
            wdq_out[side] = pair(*frame(wqg, wstat, side), biases, 0).astype(BF16)
            wret[side].start()

    for side in range(2):
        @pl.when(has[1 - side])
        def _():
            wret[side].wait_recv()
            dq_acc[...] += wdq_in[side].astype(F32)
    total = dq_acc[...]
    for step in range(1, STEPS):
        ret(jnp.int32(step)).wait_recv()
        total = total + dq_in[step].astype(F32)
    res[0] = (total.T * scale).astype(BF16)
    stores = [pltpu.make_async_copy(res.at[0], dq_hbm, local_sem.at[0])]
    stores[0].start()

    for slot in (1, 2):
        kvret[slot].wait_recv()
    dk = dk_acc[0] + kv_in[1, 0].astype(F32) + kv_in[2, 0].astype(F32)
    dv = dv_acc[0] + kv_in[1, 1].astype(F32) + kv_in[2, 1].astype(F32)
    res[1] = (dk * scale).astype(BF16)
    res[2] = dv.astype(BF16)
    for n, out in ((1, dk_hbm), (2, dv_hbm)):
        copy = pltpu.make_async_copy(res.at[n], out, local_sem.at[n])
        copy.start()
        stores.append(copy)

    for step in range(1, STEPS):
        for copy in hop[step].values():
            copy.wait_send()
        ret(jnp.int32(step)).wait_send()
    for copy in kv1 + kv2 + [kv3] + list(kvret.values()):
        copy.wait_send()
    for side in range(2):
        @pl.when(has[side])
        def _():
            for copy in win[1 - side]:
                copy.wait_send()
            wret[side].wait_send()
    for copy in stores:
        copy.wait()


def body(slab_count, space_count, query, key, value, out_saved, grad_out, log_norm, band, frames):
    any_spec = pl.BlockSpec(memory_space=pl.ANY)
    smem = pl.BlockSpec(memory_space=pltpu.SMEM)
    vmem = pl.BlockSpec(memory_space=pltpu.VMEM)
    rows = jax.ShapeDtypeStruct((ROWS, DIM), BF16)
    dma = pltpu.SemaphoreType.DMA
    return pl.pallas_call(
        functools.partial(kernel, slab_count, space_count, band.shape[0]),
        out_shape=(rows, rows, rows),
        in_specs=[any_spec] * 5 + [vmem, smem, smem],
        out_specs=[any_spec] * 3,
        scratch_shapes=[
            pltpu.VMEM((8, 2, ROWS, DIM), BF16),
            pltpu.VMEM((8, 2, 2, TILE), F32),
            pltpu.VMEM((2, 2, ROWS, DIM), BF16),
            pltpu.VMEM((2, 2, 2, TILE), F32),
            pltpu.VMEM((4, 2, ROWS, DIM), BF16),
            pltpu.VMEM((4, DIM, ROWS), BF16),
            pltpu.VMEM((ROWS, DIM), BF16),
            pltpu.VMEM((4, ROWS, DIM), F32),
            pltpu.VMEM((4, ROWS, DIM), F32),
            pltpu.VMEM((DIM, ROWS), F32),
            pltpu.VMEM((8, DIM, ROWS), BF16),
            pltpu.VMEM((8, DIM, ROWS), BF16),
            pltpu.VMEM((2, DIM, ROWS), BF16),
            pltpu.VMEM((2, DIM, ROWS), BF16),
            pltpu.VMEM((4, 2, ROWS, DIM), BF16),
            pltpu.VMEM((4, 2, ROWS, DIM), BF16),
            pltpu.VMEM((3, ROWS, DIM), BF16),
            dma((8,)),
            dma((8, 2, 3)),
            dma((8, 2, 3)),
            dma((2, 3)),
            dma((2, 3)),
            dma((5,)),
            dma((5,)),
            dma((8,)),
            dma((8,)),
            dma((2,)),
            dma((2,)),
            dma((4,)),
            dma((4,)),
        ],
        compiler_params=pltpu.CompilerParams(
            collective_id=0, has_side_effects=True, vmem_limit_bytes=63 * 1024 * 1024
        ),
    )(query, key, value, out_saved, grad_out, log_norm, band, frames)


def solution(mesh):
    rows = P(("slab", "space"), None)
    return jax.shard_map(
        functools.partial(body, mesh.shape["slab"], mesh.shape["space"]),
        mesh=mesh,
        in_specs=(rows, rows, rows, rows, rows, P(None, ("slab", "space")), P(), P()),
        out_specs=(rows, rows, rows),
        check_vma=False,
    )
```

```python
import functools
import math

import jax
import jax.numpy as jnp
from jax import lax
from jax.experimental import pallas as pl
from jax.experimental.pallas import tpu as pltpu
from jax.sharding import PartitionSpec as P

MESH = pl.DeviceIdType.MESH
TILE = 128
ROWS = 256
DIM = 128
LOG2E = math.log2(math.e)
MASKED = 1e30
BF16 = jnp.bfloat16
F32 = jnp.float32

ONWARD = {1: 3, 2: 4, 3: 5, 4: 6}
STEPS = 8


def dot_nt(a, b):
    return lax.dot_general(a, b, (((1,), (1,)), ((), ())), preferred_element_type=F32)


def dot_nn(a, b):
    return lax.dot_general(a, b, (((1,), (0,)), ((), ())), preferred_element_type=F32)


def kernel(
    slab_count,
    space_count,
    level_count,
    q_hbm,
    k_hbm,
    v_hbm,
    o_hbm,
    g_hbm,
    lse_ref,
    band,
    frames,
    dq_hbm,
    dk_hbm,
    dv_hbm,
    qg,
    stat,
    wqg,
    wstat,
    kv,
    kt,
    o_buf,
    dk_acc,
    dv_acc,
    dq_acc,
    dq_out,
    dq_in,
    wdq_out,
    wdq_in,
    kv_out,
    kv_in,
    res,
    local_sem,
    fwd_send,
    fwd_recv,
    win_send,
    win_recv,
    kv_send,
    kv_recv,
    ret_send,
    ret_recv,
    wret_send,
    wret_recv,
    kvret_send,
    kvret_recv,
):
    m = lax.axis_index("slab")
    c = lax.axis_index("space")
    group = m % 4
    base = m - group
    core = group % 2
    x_lo = group // 2
    mate = [
        m,
        base + 2 * x_lo + (1 - core),
        base + 2 * (1 - x_lo) + core,
        base + 2 * (1 - x_lo) + (1 - core),
    ]
    scale = DIM ** (-0.5)
    has = [c > 0, c < space_count - 1]
    beside = [jnp.maximum(c - 1, 0), jnp.minimum(c + 1, space_count - 1)]
    odd = c % 2 == 1

    def ring(hops):
        return (m + 4 * hops + slab_count) % slab_count

    up, down = ring(1), ring(-1)

    barrier = pltpu.get_barrier_semaphore()
    for peer in (up, down, mate[2], mate[1]):
        pl.semaphore_signal(barrier, inc=1, device_id={"slab": peer}, device_id_type=MESH)
    for side in range(2):
        @pl.when(has[side] & jnp.logical_not(odd))
        def _():
            pl.semaphore_signal(
                barrier, inc=1, device_id={"space": beside[side]}, device_id_type=MESH
            )

    loads = [
        pltpu.make_async_copy(src, dst, local_sem.at[n])
        for n, (src, dst) in enumerate(
            (
                (g_hbm, qg.at[0, 1]),
                (o_hbm, o_buf),
                (k_hbm, kv.at[0, 0]),
                (q_hbm, qg.at[0, 0]),
                (v_hbm, kv.at[0, 1]),
            )
        )
    ]
    for copy in loads:
        copy.start()

    def remote(src, dst, sems, index, peer):
        return pltpu.make_async_remote_copy(
            src_ref=src,
            dst_ref=dst,
            send_sem=sems[0].at[index],
            recv_sem=sems[1].at[index],
            device_id=peer,
            device_id_type=MESH,
        )

    fwd, kvs, wins = (fwd_send, fwd_recv), (kv_send, kv_recv), (win_send, win_recv)
    own = (q_hbm, g_hbm)

    def frame_copies(src, dst, peer, tiles=(0, 1)):
        out = {}
        for tile in tiles:
            rows = pl.ds(tile * TILE, TILE)
            for part in range(2):
                source_ref = own[part].at[rows] if src == 0 else qg.at[src, part, rows]
                out[tile, part] = remote(
                    source_ref, qg.at[dst, part, rows], fwd, (dst, tile, part), {"slab": peer}
                )
            out[tile, 2] = remote(
                stat.at[src, tile], stat.at[dst, tile], fwd, (dst, tile, 2), {"slab": peer}
            )
        return out

    hop = {}
    for s in range(1, 7):
        hop[s] = frame_copies(max(s - 2, 0), s, up if s % 2 else down)
    far = {0: frame_copies(3, 7, ring(2), (0,)), 1: frame_copies(4, 7, ring(-2), (1,))}
    hop[7] = {**far[0], **far[1]}

    def arrive(steps):
        keys = {1: ((0, 0), (0, 1), (0, 2), (1, 0), (1, 1), (1, 2))}
        keys[0] = keys[1][3:] + keys[1][:3]
        for n in range(6):
            for step in steps:
                key = keys[step % 2][n]
                hop[step][key].wait_recv()
                if step in ONWARD:
                    hop[ONWARD[step]][key].start()
                if step in (3, 4) and n < 3:
                    waiting.append(key)
            while waiting:
                hop[7][waiting.pop(0)].start()

    waiting = []

    kv1 = [remote(h, kv.at[1, n], kvs, n, {"slab": mate[1]}) for n, h in enumerate((k_hbm, v_hbm))]
    kv2 = [
        remote(h, kv.at[2, n], kvs, 2 + n, {"slab": mate[2]}) for n, h in enumerate((k_hbm, v_hbm))
    ]
    kv3 = remote(kv.at[2], kv.at[3], kvs, 4, {"slab": mate[1]})

    win = [
        [
            remote(q_hbm, wqg.at[side, 0], wins, (side, 0), {"space": beside[1 - side]}),
            remote(g_hbm, wqg.at[side, 1], wins, (side, 1), {"space": beside[1 - side]}),
            remote(stat.at[0], wstat.at[side], wins, (side, 2), {"space": beside[1 - side]}),
        ]
        for side in range(2)
    ]
    wret = [
        remote(
            wdq_out.at[side], wdq_in.at[side], (wret_send, wret_recv), side, {"space": beside[side]}
        )
        for side in range(2)
    ]

    def source(step):
        return ring(jnp.where(step % 2 == 1, -1, 1) * ((step + 1) // 2))

    def ret(step):
        return remote(
            dq_out.at[step], dq_in.at[step], (ret_send, ret_recv), step, {"slab": source(step)}
        )

    kvret = {
        slot: remote(
            kv_out.at[slot], kv_in.at[slot], (kvret_send, kvret_recv), slot, {"slab": mate[peer]}
        )
        for slot, peer in ((1, 1), (2, 2), (3, 1))
    }

    pl.semaphore_wait(
        barrier, 4 + jnp.where(odd, has[0].astype(jnp.int32) + has[1].astype(jnp.int32), 0)
    )

    for key in ((0, 0), (0, 1), (1, 0), (1, 1)):
        hop[1][key].start()
        hop[2][key].start()
    for copy in kv2 + kv1:
        copy.start()

    for copy in loads[:2]:
        copy.wait()
    for t in range(2):
        rows = pl.ds(t * TILE, TILE)
        product = qg[0, 1, rows, :].astype(F32) * o_buf[rows, :].astype(F32)
        stat[0, t, 1:2, :] = jnp.sum(product.T, axis=0, keepdims=True)
        stat[0, t, 0:1, :] = lse_ref[:, t * TILE : (t + 1) * TILE] * LOG2E
    for tile in range(2):
        hop[1][tile, 2].start()
        hop[2][tile, 2].start()

    def win_start(side):
        for copy in win[side]:
            copy.start()

    for side in range(2):
        @pl.when(odd & has[1 - side])
        def _():
            win_start(side)

    for copy in loads[2:]:
        copy.wait()

    lane = lax.broadcasted_iota(jnp.int32, (1, ROWS), 1)

    def mask_bias(level, q_tile, k_tile):
        return jnp.where(band[level, q_tile, k_tile] > 0, 0.0, MASKED).astype(F32)

    def level_between(a, b):
        distance = jnp.abs(frames[a] - frames[b])
        level = jnp.int32(0)
        for n in range(level_count - 1):
            level = level + jnp.where(distance >= 2**n, 1, 0)
        return level

    def key_t(j):
        kt[j] = kv[j, 0].astype(F32).T.astype(BF16)

    def pair(q, g, lse, delta, biases, j, fresh=False):
        key = kv[j, 0]
        shift = [lse + jnp.where(lane < TILE, biases[t][0], biases[t][1]) for t in range(2)]
        shifts = jnp.concatenate(
            [jnp.broadcast_to(shift[t], (TILE, ROWS)) for t in range(2)], axis=0
        )
        prob = jnp.exp2(dot_nt(key, q) * (scale * LOG2E) - shifts)
        dprob = dot_nt(kv[j, 1], g)
        dscore = (prob * (dprob - delta)).astype(BF16)
        dv = dot_nn(prob.astype(BF16), g)
        dk = dot_nn(dscore, q)
        dv_acc[j] = dv if fresh else dv_acc[j] + dv
        dk_acc[j] = dk if fresh else dk_acc[j] + dk
        return dot_nn(kt[j], dscore)

    def frame(block, rows, s):
        return [block[s, 0], block[s, 1]] + [
            jnp.concatenate([rows[s, 0, n : n + 1, :], rows[s, 1, n : n + 1, :]], axis=1)
            for n in range(2)
        ]

    def visit(s, j, fresh=False):
        level = level_between(source(s), mate[j]) if not fresh else level_between(m, mate[j])
        biases = [[mask_bias(level, 2 * c + h, 2 * c + t) for h in range(2)] for t in range(2)]
        return pair(*frame(qg, stat, s), biases, j, fresh)

    def window(side):
        @pl.when(odd)
        def _():
            for copy in win[side]:
                copy.wait_recv()

        biases = [
            [mask_bias(0, 2 * beside[side] + h, 2 * c + t) for h in range(2)] for t in range(2)
        ]
        wdq_out[side] = pair(*frame(wqg, wstat, side), biases, 0).astype(BF16)
        wret[side].start()

    key_t(0)
    dq_acc[...] = visit(0, 0, True)
    for copy in kv1:
        copy.wait_recv()
    key_t(1)
    dq_acc[...] += visit(0, 1, True)
    arrive((1, 2))
    for copy in kv2:
        copy.wait_recv()
    kv3.start()
    key_t(2)
    dq_acc[...] += visit(0, 2, True)
    kv3.wait_recv()
    key_t(3)
    dq_acc[...] += visit(0, 3, True)

    def turn(s, carry):
        @pl.when(s == 2)
        def _():
            arrive((3, 4))

        for n in (5, 6):
            @pl.when(s == n)
            def _():
                arrive((n,))

        for side, n in ((1, 3), (0, 4)):
            @pl.when((s == n) & has[side] & jnp.logical_not(odd))
            def _():
                for copy in win[side]:
                    copy.wait_recv()
                win_start(1 - side)

        for side in range(2):
            @pl.when((s == 6) & has[side])
            def _():
                window(side)

        total = visit(s, 0)
        for j in range(1, 4):
            total = total + visit(s, j)
        dq_out[s] = total.astype(BF16)
        ret(s).start()
        return carry

    lax.fori_loop(1, STEPS - 1, turn, 0)

    def pack(j, extra=None):
        dk = dk_acc[j]
        dv = dv_acc[j]
        if extra is not None:
            dk = dk + kv_in[extra, 0].astype(F32)
            dv = dv + kv_in[extra, 1].astype(F32)
        kv_out[j, 0] = dk.astype(BF16)
        kv_out[j, 1] = dv.astype(BF16)

    last = jnp.int32(STEPS - 1)
    arrive((7,))
    total = visit(last, 3)
    pack(3)
    kvret[3].start()
    for j in (2, 1, 0):
        total = total + visit(last, j)
    dq_out[last] = total.astype(BF16)
    ret(last).start()
    pack(1)
    kvret[1].start()
    kvret[3].wait_recv()
    pack(2, 3)
    kvret[2].start()

    for side in range(2):
        @pl.when(has[1 - side])
        def _():
            wret[side].wait_recv()
            dq_acc[...] += wdq_in[side].astype(F32)
    total = dq_acc[...]
    for step in range(1, STEPS):
        ret(jnp.int32(step)).wait_recv()
        total = total + dq_in[step].astype(F32)
    dq_hbm[...] = (total.T * scale).astype(BF16)

    for slot in (1, 2):
        kvret[slot].wait_recv()
    dk = dk_acc[0] + kv_in[1, 0].astype(F32) + kv_in[2, 0].astype(F32)
    dv = dv_acc[0] + kv_in[1, 1].astype(F32) + kv_in[2, 1].astype(F32)
    dk_hbm[...] = (dk * scale).astype(BF16)
    dv_hbm[...] = dv.astype(BF16)

    for step in range(1, STEPS):
        for copy in hop[step].values():
            copy.wait_send()
        ret(jnp.int32(step)).wait_send()
    for copy in kv1 + kv2 + [kv3] + list(kvret.values()):
        copy.wait_send()
    for side in range(2):
        @pl.when(has[side])
        def _():
            for copy in win[1 - side]:
                copy.wait_send()
            wret[side].wait_send()


def body(slab_count, space_count, query, key, value, out_saved, grad_out, log_norm, band, frames):
    any_spec = pl.BlockSpec(memory_space=pl.ANY)
    smem = pl.BlockSpec(memory_space=pltpu.SMEM)
    vmem = pl.BlockSpec(memory_space=pltpu.VMEM)
    rows = jax.ShapeDtypeStruct((ROWS, DIM), BF16)
    dma = pltpu.SemaphoreType.DMA
    return pl.pallas_call(
        functools.partial(kernel, slab_count, space_count, band.shape[0]),
        out_shape=(rows, rows, rows),
        in_specs=[any_spec] * 5 + [vmem, smem, smem],
        out_specs=[vmem] * 3,
        scratch_shapes=[
            pltpu.VMEM((8, 2, ROWS, DIM), BF16),
            pltpu.VMEM((8, 2, 2, TILE), F32),
            pltpu.VMEM((2, 2, ROWS, DIM), BF16),
            pltpu.VMEM((2, 2, 2, TILE), F32),
            pltpu.VMEM((4, 2, ROWS, DIM), BF16),
            pltpu.VMEM((4, DIM, ROWS), BF16),
            pltpu.VMEM((ROWS, DIM), BF16),
            pltpu.VMEM((4, ROWS, DIM), F32),
            pltpu.VMEM((4, ROWS, DIM), F32),
            pltpu.VMEM((DIM, ROWS), F32),
            pltpu.VMEM((8, DIM, ROWS), BF16),
            pltpu.VMEM((8, DIM, ROWS), BF16),
            pltpu.VMEM((2, DIM, ROWS), BF16),
            pltpu.VMEM((2, DIM, ROWS), BF16),
            pltpu.VMEM((4, 2, ROWS, DIM), BF16),
            pltpu.VMEM((4, 2, ROWS, DIM), BF16),
            pltpu.VMEM((3, ROWS, DIM), BF16),
            dma((8,)),
            dma((8, 2, 3)),
            dma((8, 2, 3)),
            dma((2, 3)),
            dma((2, 3)),
            dma((5,)),
            dma((5,)),
            dma((8,)),
            dma((8,)),
            dma((2,)),
            dma((2,)),
            dma((4,)),
            dma((4,)),
        ],
        compiler_params=pltpu.CompilerParams(
            collective_id=0, has_side_effects=True, vmem_limit_bytes=24 * 1024 * 1024
        ),
    )(*[pltpu.with_memory_space_constraint(a, pltpu.HBM) for a in (query, key, value, out_saved, grad_out, log_norm, band, frames)])


def solution(mesh):
    rows = P(("slab", "space"), None)
    return jax.shard_map(
        functools.partial(body, mesh.shape["slab"], mesh.shape["space"]),
        mesh=mesh,
        in_specs=(rows, rows, rows, rows, rows, P(None, ("slab", "space")), P(), P()),
        out_specs=(rows, rows, rows),
        check_vma=False,
    )
```

```python
import functools
import math

import jax
import jax.numpy as jnp
from jax import lax
from jax.experimental import pallas as pl
from jax.experimental.pallas import tpu as pltpu
from jax.sharding import PartitionSpec as P

MESH = pl.DeviceIdType.MESH
TILE = 128
ROWS = 256
DIM = 128
LOG2E = math.log2(math.e)
MASKED = 1e30
BF16 = jnp.bfloat16
F32 = jnp.float32

ONWARD = {1: 3, 2: 4, 3: 5, 4: 6}
STEPS = 8


def dot_nt(a, b):
    return lax.dot_general(a, b, (((1,), (1,)), ((), ())), preferred_element_type=F32)


def dot_nn(a, b):
    return lax.dot_general(a, b, (((1,), (0,)), ((), ())), preferred_element_type=F32)


def kernel(
    slab_count,
    space_count,
    level_count,
    q_hbm,
    k_hbm,
    v_hbm,
    o_hbm,
    g_hbm,
    lse_ref,
    band,
    frames,
    dq_ref,
    dk_ref,
    dv_ref,
    qg,
    stat,
    wqg,
    wstat,
    kv,
    kt,
    o_buf,
    dk_acc,
    dv_acc,
    dq_acc,
    dq_out,
    dq_in,
    dq_mid,
    dq7_out,
    dq7_in,
    wdq_out,
    wdq_in,
    kv_out,
    kv_in,
    local_sem,
    fwd_send,
    fwd_recv,
    win_send,
    win_recv,
    kv_send,
    kv_recv,
    ret_send,
    ret_recv,
    wret_send,
    wret_recv,
    kvret_send,
    kvret_recv,
    in_sem,
):
    m = lax.axis_index("slab")
    c = lax.axis_index("space")
    group = m % 4
    base = m - group
    core = group % 2
    x_lo = group // 2
    mate = [
        m,
        base + 2 * x_lo + (1 - core),
        base + 2 * (1 - x_lo) + core,
        base + 2 * (1 - x_lo) + (1 - core),
    ]
    scale = DIM ** (-0.5)
    has = [c > 0, c < space_count - 1]
    beside = [jnp.maximum(c - 1, 0), jnp.minimum(c + 1, space_count - 1)]
    odd = c % 2 == 1

    def ring(hops):
        return (m + 4 * hops + slab_count) % slab_count

    up, down = ring(1), ring(-1)

    barrier = pltpu.get_barrier_semaphore()
    for peer in (up, down, mate[2], mate[1]):
        pl.semaphore_signal(barrier, inc=1, device_id={"slab": peer}, device_id_type=MESH)
    for side in range(2):
        @pl.when(has[side] & jnp.logical_not(odd))
        def _():
            pl.semaphore_signal(
                barrier, inc=1, device_id={"space": beside[side]}, device_id_type=MESH
            )

    loads = [
        pltpu.make_async_copy(src, dst, local_sem.at[n])
        for n, (src, dst) in enumerate(
            (
                (g_hbm, qg.at[0, 1]),
                (o_hbm, o_buf),
                (k_hbm, kv.at[0, 0]),
                (q_hbm, qg.at[0, 0]),
                (v_hbm, kv.at[0, 1]),
            )
        )
    ]
    for copy in loads:
        copy.start()

    def remote(src, dst, sems, index, peer):
        return pltpu.make_async_remote_copy(
            src_ref=src,
            dst_ref=dst,
            send_sem=sems[0].at[index],
            recv_sem=sems[1].at[index],
            device_id=peer,
            device_id_type=MESH,
        )

    fwd, kvs, wins = (fwd_send, fwd_recv), (kv_send, kv_recv), (win_send, win_recv)
    own = (q_hbm, g_hbm)

    def frame_copies(src, dst, peer, tiles=(0, 1)):
        out = {}
        for tile in tiles:
            rows = pl.ds(tile * TILE, TILE)
            for part in range(2):
                source_ref = own[part].at[rows] if src == 0 else qg.at[src, part, rows]
                out[tile, part] = remote(
                    source_ref, qg.at[dst, part, rows], fwd, (dst, tile, part), {"slab": peer}
                )
            out[tile, 2] = remote(
                stat.at[src, tile], stat.at[dst, tile], fwd, (dst, tile, 2), {"slab": peer}
            )
        return out

    hop = {}
    for s in range(1, 7):
        hop[s] = frame_copies(max(s - 2, 0), s, up if s % 2 else down)
    far = {0: frame_copies(3, 7, ring(2), (0,)), 1: frame_copies(4, 7, ring(-2), (1,))}
    hop[7] = {**far[0], **far[1]}

    def arrive(steps):
        keys = {1: ((0, 0), (0, 1), (0, 2), (1, 0), (1, 1), (1, 2))}
        keys[0] = keys[1][3:] + keys[1][:3]
        for n in range(6):
            for step in steps:
                key = keys[step % 2][n]
                hop[step][key].wait_recv()
                if step in ONWARD:
                    hop[ONWARD[step]][key].start()
                if step in (3, 4) and n < 3:
                    waiting.append(key)
            while waiting:
                hop[7][waiting.pop(0)].start()

    waiting = []

    kv1 = [remote(h, kv.at[1, n], kvs, n, {"slab": mate[1]}) for n, h in enumerate((k_hbm, v_hbm))]
    kv2 = [
        remote(h, kv.at[2, n], kvs, 2 + n, {"slab": mate[2]}) for n, h in enumerate((k_hbm, v_hbm))
    ]
    kv3 = remote(kv.at[2], kv.at[3], kvs, 4, {"slab": mate[1]})

    win = [
        [
            remote(q_hbm, wqg.at[side, 0], wins, (side, 0), {"space": beside[1 - side]}),
            remote(g_hbm, wqg.at[side, 1], wins, (side, 1), {"space": beside[1 - side]}),
            remote(stat.at[0], wstat.at[side], wins, (side, 2), {"space": beside[1 - side]}),
        ]
        for side in range(2)
    ]
    wret = [
        remote(
            wdq_out.at[side], wdq_in.at[side], (wret_send, wret_recv), side, {"space": beside[side]}
        )
        for side in range(2)
    ]

    def source(step):
        return ring(jnp.where(step % 2 == 1, -1, 1) * ((step + 1) // 2))

    rets = (ret_send, ret_recv)

    def side_of(step):
        return jnp.where(step % 2 == 1, -1, 1)

    def ret(step, hops=1):
        return remote(
            dq_out.at[step], dq_in.at[step], rets, step, {"slab": ring(side_of(step) * hops)}
        )

    def ret7(tile):
        return remote(
            dq7_out.at[tile], dq7_in.at[tile], rets, 7 + tile, {"slab": ring(-2 if tile == 0 else 2)}
        )

    kvret = {
        (slot, n): remote(
            kv_out.at[slot, n],
            kv_in.at[slot, n],
            (kvret_send, kvret_recv),
            (slot, n),
            {"slab": mate[peer]},
        )
        for slot, peer in ((1, 1), (2, 2), (3, 1))
        for n in range(2)
    }

    pl.semaphore_wait(
        barrier, 4 + jnp.where(odd, has[0].astype(jnp.int32) + has[1].astype(jnp.int32), 0)
    )

    for side in range(2):
        @pl.when(odd & has[side])
        def _():
            pl.semaphore_signal(
                in_sem.at[1 - side],
                inc=1,
                device_id={"space": beside[side]},
                device_id_type=MESH,
            )

    for key in ((0, 0), (0, 1), (1, 0), (1, 1)):
        hop[1][key].start()
        hop[2][key].start()
    for copy in kv2 + kv1:
        copy.start()

    for copy in loads[:2]:
        copy.wait()
    for t in range(2):
        rows = pl.ds(t * TILE, TILE)
        product = qg[0, 1, rows, :].astype(F32) * o_buf[rows, :].astype(F32)
        stat[0, t, 1:2, :] = jnp.sum(product.T, axis=0, keepdims=True)
        stat[0, t, 0:1, :] = lse_ref[:, t * TILE : (t + 1) * TILE] * LOG2E
    for tile in range(2):
        hop[1][tile, 2].start()
        hop[2][tile, 2].start()

    def win_start(side):
        for copy in win[side]:
            copy.start()

    for side in range(2):
        @pl.when(odd & has[1 - side])
        def _():
            win_start(side)

    for copy in loads[2:]:
        copy.wait()

    lane = lax.broadcasted_iota(jnp.int32, (1, ROWS), 1)

    def mask_bias(level, q_tile, k_tile):
        return jnp.where(band[level, q_tile, k_tile] > 0, 0.0, MASKED).astype(F32)

    def level_between(a, b):
        distance = jnp.abs(frames[a] - frames[b])
        level = jnp.int32(0)
        for n in range(level_count - 1):
            level = level + jnp.where(distance >= 2**n, 1, 0)
        return level

    def key_t(j):
        kt[j] = kv[j, 0].astype(F32).T.astype(BF16)

    def pair(q, g, lse, delta, biases, j, fresh=False):
        key = kv[j, 0]
        shift = [lse + jnp.where(lane < TILE, biases[t][0], biases[t][1]) for t in range(2)]
        shifts = jnp.concatenate(
            [jnp.broadcast_to(shift[t], (TILE, ROWS)) for t in range(2)], axis=0
        )
        prob = jnp.exp2(dot_nt(key, q) * (scale * LOG2E) - shifts)
        dprob = dot_nt(kv[j, 1], g)
        dscore = (prob * (dprob - delta)).astype(BF16)
        dv = dot_nn(prob.astype(BF16), g)
        dk = dot_nn(dscore, q)
        dv_acc[j] = dv if fresh else dv_acc[j] + dv
        dk_acc[j] = dk if fresh else dk_acc[j] + dk
        return dot_nn(kt[j], dscore)

    def frame(block, rows, s):
        return [block[s, 0], block[s, 1]] + [
            jnp.concatenate([rows[s, 0, n : n + 1, :], rows[s, 1, n : n + 1, :]], axis=1)
            for n in range(2)
        ]

    def visit(s, j, fresh=False):
        level = level_between(source(s), mate[j]) if not fresh else level_between(m, mate[j])
        biases = [[mask_bias(level, 2 * c + h, 2 * c + t) for h in range(2)] for t in range(2)]
        return pair(*frame(qg, stat, s), biases, j, fresh)

    def window(side):
        for copy in win[side]:
            copy.wait_recv()

        biases = [
            [mask_bias(0, 2 * beside[side] + h, 2 * c + t) for h in range(2)] for t in range(2)
        ]
        wdq_out[side] = pair(*frame(wqg, wstat, side), biases, 0).astype(BF16)
        wret[side].start()

    def visit_all(s):
        q, g, lse, delta = frame(qg, stat, s)
        keys = jnp.concatenate([kv[j, 0] for j in range(4)], axis=0)
        values = jnp.concatenate([kv[j, 1] for j in range(4)], axis=0)
        scores = dot_nt(keys, q)
        dprobs = dot_nt(values, g)
        probs, dscores = [], []
        for j in range(4):
            level = level_between(source(s), mate[j])
            for t in range(2):
                bias = [mask_bias(level, 2 * c + h, 2 * c + t) for h in range(2)]
                shift = lse + jnp.where(lane < TILE, bias[0], bias[1])
                at = (2 * j + t) * TILE
                prob = jnp.exp2(scores[at : at + TILE] * (scale * LOG2E) - shift)
                probs.append(prob.astype(BF16))
                dscores.append((prob * (dprobs[at : at + TILE] - delta)).astype(BF16))
        prob = jnp.concatenate(probs, axis=0)
        dscore = jnp.concatenate(dscores, axis=0)
        dv = dot_nn(prob, g)
        dk = dot_nn(dscore, q)
        for j in range(4):
            dv_acc[j] += dv[j * ROWS : (j + 1) * ROWS]
            dk_acc[j] += dk[j * ROWS : (j + 1) * ROWS]
        kt_all = jnp.concatenate([kt[j] for j in range(4)], axis=1)
        return dot_nn(kt_all, dscore)

    even = jnp.logical_not(odd)
    far_left = even & has[0] & (c % (space_count // 2) == 0)

    def answer(side):
        pl.semaphore_wait(in_sem.at[side], 1)
        win_start(1 - side)

    key_t(0)
    dq_acc[...] = visit(0, 0, True)

    @pl.when(even & has[0] & (c % (space_count // 2) != 0))
    def _():
        answer(0)

    for copy in kv1:
        copy.wait_recv()
    key_t(1)
    dq_acc[...] += visit(0, 1, True)
    arrive((1, 2))

    @pl.when(even & has[1])
    def _():
        answer(1)

    for copy in kv2:
        copy.wait_recv()
    kv3.start()
    key_t(2)
    dq_acc[...] += visit(0, 2, True)
    kv3.wait_recv()
    key_t(3)
    dq_acc[...] += visit(0, 3, True)

    def turn(turn_index, carry):
        s = turn_index
        @pl.when(s == 2)
        def _():
            arrive((3, 4))

        @pl.when((s == 4) & far_left)
        def _():
            answer(0)

        for side in range(2):
            @pl.when((s == 6) & has[side])
            def _():
                window(side)

        for n in (5, 6, 7):
            @pl.when(s == n)
            def _():
                arrive((n,))

        total = visit_all(s)
        middle = (s == 3) | (s == 4)

        @pl.when(middle)
        def _():
            dq_mid[s - 3] = total

        @pl.when(s == 7)
        def _():
            for tile in range(2):
                dq7_out[tile] = total[:, tile * TILE : (tile + 1) * TILE].astype(BF16)
                ret7(tile).start()

        @pl.when(jnp.logical_not(middle | (s == 7)))
        def _():
            dq_out[s] = total.astype(BF16)
            ret(s).start()

        return carry

    lax.fori_loop(1, STEPS, turn, 0)

    sums = (dk_acc, dv_acc)

    def give(j, extra=None):
        for n in range(2):
            part = sums[n][j]
            if extra is not None:
                kvret[extra, n].wait_recv()
                part = part + kv_in[extra, n].astype(F32)
            kv_out[j, n] = part.astype(BF16)
            kvret[j, n].start()

    give(3)
    give(1)
    give(2, 3)

    for n in range(2):
        ret(jnp.int32(5 + n)).wait_recv()
        part = dq_mid[n] + dq_in[5 + n].astype(F32)
        ret7(n).wait_recv()
        far_part = dq7_in[n].astype(F32)
        halves = [part[:, :TILE], part[:, TILE:]]
        halves[n] = halves[n] + far_part
        for tile in range(2):
            dq_out[3 + n, :, tile * TILE : (tile + 1) * TILE] = halves[tile].astype(BF16)
        ret(jnp.int32(3 + n), 2).start()

    for side in range(2):
        @pl.when(has[1 - side])
        def _():
            wret[side].wait_recv()
            dq_acc[...] += wdq_in[side].astype(F32)
    total = dq_acc[...]
    for step in range(1, 5):
        ret(jnp.int32(step), (step + 1) // 2).wait_recv()
        total = total + dq_in[step].astype(F32)
    dq_ref[...] = (total.T * scale).astype(BF16)

    for n, out in ((0, dk_ref), (1, dv_ref)):
        part = sums[n][0]
        for slot in (1, 2):
            kvret[slot, n].wait_recv()
            part = part + kv_in[slot, n].astype(F32)
        out[...] = (part * scale if n == 0 else part).astype(BF16)

    for step in range(1, STEPS):
        for copy in hop[step].values():
            copy.wait_send()
        if step < 7:
            ret(jnp.int32(step), 2 if step in (3, 4) else 1).wait_send()
    for tile in range(2):
        ret7(tile).wait_send()
    for copy in kv1 + kv2 + [kv3] + list(kvret.values()):
        copy.wait_send()
    for side in range(2):
        @pl.when(has[side])
        def _():
            for copy in win[1 - side]:
                copy.wait_send()
            wret[side].wait_send()


def body(slab_count, space_count, query, key, value, out_saved, grad_out, log_norm, band, frames):
    any_spec = pl.BlockSpec(memory_space=pl.ANY)
    smem = pl.BlockSpec(memory_space=pltpu.SMEM)
    vmem = pl.BlockSpec(memory_space=pltpu.VMEM)
    rows = jax.ShapeDtypeStruct((ROWS, DIM), BF16)
    dma = pltpu.SemaphoreType.DMA
    return pl.pallas_call(
        functools.partial(kernel, slab_count, space_count, band.shape[0]),
        out_shape=(rows, rows, rows),
        in_specs=[any_spec] * 5 + [vmem, smem, smem],
        out_specs=[vmem] * 3,
        scratch_shapes=[
            pltpu.VMEM((8, 2, ROWS, DIM), BF16),
            pltpu.VMEM((8, 2, 2, TILE), F32),
            pltpu.VMEM((2, 2, ROWS, DIM), BF16),
            pltpu.VMEM((2, 2, 2, TILE), F32),
            pltpu.VMEM((4, 2, ROWS, DIM), BF16),
            pltpu.VMEM((4, DIM, ROWS), BF16),
            pltpu.VMEM((ROWS, DIM), BF16),
            pltpu.VMEM((4, ROWS, DIM), F32),
            pltpu.VMEM((4, ROWS, DIM), F32),
            pltpu.VMEM((DIM, ROWS), F32),
            pltpu.VMEM((8, DIM, ROWS), BF16),
            pltpu.VMEM((8, DIM, ROWS), BF16),
            pltpu.VMEM((2, DIM, ROWS), F32),
            pltpu.VMEM((2, DIM, TILE), BF16),
            pltpu.VMEM((2, DIM, TILE), BF16),
            pltpu.VMEM((2, DIM, ROWS), BF16),
            pltpu.VMEM((2, DIM, ROWS), BF16),
            pltpu.VMEM((4, 2, ROWS, DIM), BF16),
            pltpu.VMEM((4, 2, ROWS, DIM), BF16),
            dma((8,)),
            dma((8, 2, 3)),
            dma((8, 2, 3)),
            dma((2, 3)),
            dma((2, 3)),
            dma((5,)),
            dma((5,)),
            dma((9,)),
            dma((9,)),
            dma((2,)),
            dma((2,)),
            dma((4, 2)),
            dma((4, 2)),
            pltpu.SemaphoreType.REGULAR((2,)),
        ],
        compiler_params=pltpu.CompilerParams(
            collective_id=0, has_side_effects=True, vmem_limit_bytes=24 * 1024 * 1024
        ),
    )(*[pltpu.with_memory_space_constraint(a, pltpu.HBM) for a in (query, key, value, out_saved, grad_out, log_norm, band, frames)])


def solution(mesh):
    rows = P(("slab", "space"), None)
    return jax.shard_map(
        functools.partial(body, mesh.shape["slab"], mesh.shape["space"]),
        mesh=mesh,
        in_specs=(rows, rows, rows, rows, rows, P(None, ("slab", "space")), P(), P()),
        out_specs=(rows, rows, rows),
        check_vma=False,
    )
```

```python
import functools
import math

import jax
import jax.numpy as jnp
from jax import lax
from jax.experimental import pallas as pl
from jax.experimental.pallas import tpu as pltpu
from jax.sharding import PartitionSpec as P

MESH = pl.DeviceIdType.MESH
TILE = 128
ROWS = 256
DIM = 128
LOG2E = math.log2(math.e)
MASKED = 1e30
BF16 = jnp.bfloat16
F32 = jnp.float32

ONWARD = {1: 3, 2: 4, 3: 5, 4: 6}
STEPS = 8


def dot_nt(a, b):
    return lax.dot_general(a, b, (((1,), (1,)), ((), ())), preferred_element_type=F32)


def dot_nn(a, b):
    return lax.dot_general(a, b, (((1,), (0,)), ((), ())), preferred_element_type=F32)


def kernel(
    slab_count,
    space_count,
    level_count,
    q_hbm,
    k_hbm,
    v_hbm,
    o_hbm,
    g_hbm,
    lse_ref,
    band,
    frames,
    out_ref,
    qg,
    stat,
    wqg,
    wstat,
    kv,
    kt,
    o_buf,
    dk_acc,
    dv_acc,
    dq_acc,
    dq_out,
    dq_in,
    dq_mid,
    dq7_out,
    dq7_in,
    wdq_out,
    wdq_in,
    kv_out,
    kv_in,
    local_sem,
    fwd_send,
    fwd_recv,
    win_send,
    win_recv,
    kv_send,
    kv_recv,
    ret_send,
    ret_recv,
    wret_send,
    wret_recv,
    kvret_send,
    kvret_recv,
    in_sem,
):
    m = lax.axis_index("slab")
    c = lax.axis_index("space")
    group = m % 4
    base = m - group
    core = group % 2
    x_lo = group // 2
    mate = [
        m,
        base + 2 * x_lo + (1 - core),
        base + 2 * (1 - x_lo) + core,
        base + 2 * (1 - x_lo) + (1 - core),
    ]
    scale = DIM ** (-0.5)
    has = [c > 0, c < space_count - 1]
    beside = [jnp.maximum(c - 1, 0), jnp.minimum(c + 1, space_count - 1)]
    odd = c % 2 == 1

    def ring(hops):
        return (m + 4 * hops + slab_count) % slab_count

    up, down = ring(1), ring(-1)

    barrier = pltpu.get_barrier_semaphore()
    for peer in (up, down, mate[2], mate[1]):
        pl.semaphore_signal(barrier, inc=1, device_id={"slab": peer}, device_id_type=MESH)
    for side in range(2):
        @pl.when(has[side] & jnp.logical_not(odd))
        def _():
            pl.semaphore_signal(
                barrier, inc=1, device_id={"space": beside[side]}, device_id_type=MESH
            )

    loads = [
        pltpu.make_async_copy(src, dst, local_sem.at[n])
        for n, (src, dst) in enumerate(
            (
                (g_hbm, qg.at[0, 1]),
                (o_hbm, o_buf),
                (k_hbm, kv.at[0, 0]),
                (q_hbm, qg.at[0, 0]),
                (v_hbm, kv.at[0, 1]),
            )
        )
    ]
    for copy in loads:
        copy.start()

    def remote(src, dst, sems, index, peer):
        return pltpu.make_async_remote_copy(
            src_ref=src,
            dst_ref=dst,
            send_sem=sems[0].at[index],
            recv_sem=sems[1].at[index],
            device_id=peer,
            device_id_type=MESH,
        )

    fwd, kvs, wins = (fwd_send, fwd_recv), (kv_send, kv_recv), (win_send, win_recv)
    own = (q_hbm, g_hbm)

    def frame_copies(src, dst, peer, tiles=(0, 1)):
        out = {}
        for tile in tiles:
            rows = pl.ds(tile * TILE, TILE)
            for part in range(2):
                source_ref = own[part].at[rows] if src == 0 else qg.at[src, part, rows]
                out[tile, part] = remote(
                    source_ref, qg.at[dst, part, rows], fwd, (dst, tile, part), {"slab": peer}
                )
            out[tile, 2] = remote(
                stat.at[src, tile], stat.at[dst, tile], fwd, (dst, tile, 2), {"slab": peer}
            )
        return out

    hop = {}
    for s in range(1, 7):
        hop[s] = frame_copies(max(s - 2, 0), s, up if s % 2 else down)
    far = {0: frame_copies(3, 7, ring(2), (0,)), 1: frame_copies(4, 7, ring(-2), (1,))}
    hop[7] = {**far[0], **far[1]}

    def arrive(steps):
        keys = {1: ((0, 0), (0, 1), (0, 2), (1, 0), (1, 1), (1, 2))}
        keys[0] = keys[1][3:] + keys[1][:3]
        for n in range(6):
            for step in steps:
                key = keys[step % 2][n]
                hop[step][key].wait_recv()
                if step in ONWARD:
                    hop[ONWARD[step]][key].start()
                if step in (3, 4) and n < 3:
                    waiting.append(key)
            while waiting:
                hop[7][waiting.pop(0)].start()

    waiting = []

    kv1 = [remote(h, kv.at[1, n], kvs, n, {"slab": mate[1]}) for n, h in enumerate((k_hbm, v_hbm))]
    kv2 = [
        remote(h, kv.at[2, n], kvs, 2 + n, {"slab": mate[2]}) for n, h in enumerate((k_hbm, v_hbm))
    ]
    kv3 = remote(kv.at[2], kv.at[3], kvs, 4, {"slab": mate[1]})

    win = [
        [
            remote(q_hbm, wqg.at[side, 0], wins, (side, 0), {"space": beside[1 - side]}),
            remote(g_hbm, wqg.at[side, 1], wins, (side, 1), {"space": beside[1 - side]}),
            remote(stat.at[0], wstat.at[side], wins, (side, 2), {"space": beside[1 - side]}),
        ]
        for side in range(2)
    ]
    wret = [
        remote(
            wdq_out.at[side], wdq_in.at[side], (wret_send, wret_recv), side, {"space": beside[side]}
        )
        for side in range(2)
    ]

    def source(step):
        return ring(jnp.where(step % 2 == 1, -1, 1) * ((step + 1) // 2))

    rets = (ret_send, ret_recv)

    def side_of(step):
        return jnp.where(step % 2 == 1, -1, 1)

    def ret(step, hops=1):
        return remote(
            dq_out.at[step], dq_in.at[step], rets, step, {"slab": ring(side_of(step) * hops)}
        )

    def ret7(tile):
        return remote(
            dq7_out.at[tile], dq7_in.at[tile], rets, 7 + tile, {"slab": ring(-2 if tile == 0 else 2)}
        )

    kvret = {
        (slot, n): remote(
            kv_out.at[slot, n],
            kv_in.at[slot, n],
            (kvret_send, kvret_recv),
            (slot, n),
            {"slab": mate[peer]},
        )
        for slot, peer in ((1, 1), (2, 2), (3, 1))
        for n in range(2)
    }

    pl.semaphore_wait(
        barrier, 4 + jnp.where(odd, has[0].astype(jnp.int32) + has[1].astype(jnp.int32), 0)
    )

    for side in range(2):
        @pl.when(odd & has[side])
        def _():
            pl.semaphore_signal(
                in_sem.at[1 - side],
                inc=1,
                device_id={"space": beside[side]},
                device_id_type=MESH,
            )

    for key in ((0, 0), (0, 1), (1, 0), (1, 1)):
        hop[1][key].start()
        hop[2][key].start()
    for copy in kv2 + kv1:
        copy.start()

    for copy in loads[:2]:
        copy.wait()
    for t in range(2):
        rows = pl.ds(t * TILE, TILE)
        product = qg[0, 1, rows, :].astype(F32) * o_buf[rows, :].astype(F32)
        stat[0, t, 1:2, :] = jnp.sum(product.T, axis=0, keepdims=True)
        stat[0, t, 0:1, :] = lse_ref[:, t * TILE : (t + 1) * TILE] * LOG2E
    for tile in range(2):
        hop[1][tile, 2].start()
        hop[2][tile, 2].start()

    def win_start(side):
        for copy in win[side]:
            copy.start()

    for side in range(2):
        @pl.when(odd & has[1 - side])
        def _():
            win_start(side)

    for copy in loads[2:]:
        copy.wait()

    lane = lax.broadcasted_iota(jnp.int32, (1, ROWS), 1)

    def mask_bias(level, q_tile, k_tile):
        return jnp.where(band[level, q_tile, k_tile] > 0, 0.0, MASKED).astype(F32)

    def level_between(a, b):
        distance = jnp.abs(frames[a] - frames[b])
        level = jnp.int32(0)
        for n in range(level_count - 1):
            level = level + jnp.where(distance >= 2**n, 1, 0)
        return level

    def key_t(j):
        kt[j] = kv[j, 0].astype(F32).T.astype(BF16)

    def pair(q, g, lse, delta, biases, j, fresh=False):
        key = kv[j, 0]
        shift = [lse + jnp.where(lane < TILE, biases[t][0], biases[t][1]) for t in range(2)]
        shifts = jnp.concatenate(
            [jnp.broadcast_to(shift[t], (TILE, ROWS)) for t in range(2)], axis=0
        )
        prob = jnp.exp2(dot_nt(key, q) * (scale * LOG2E) - shifts)
        dprob = dot_nt(kv[j, 1], g)
        dscore = (prob * (dprob - delta)).astype(BF16)
        dv = dot_nn(prob.astype(BF16), g)
        dk = dot_nn(dscore, q)
        dv_acc[j] = dv if fresh else dv_acc[j] + dv
        dk_acc[j] = dk if fresh else dk_acc[j] + dk
        return dot_nn(kt[j], dscore)

    def frame(block, rows, s):
        return [block[s, 0], block[s, 1]] + [
            jnp.concatenate([rows[s, 0, n : n + 1, :], rows[s, 1, n : n + 1, :]], axis=1)
            for n in range(2)
        ]

    def visit(s, j, fresh=False):
        level = level_between(source(s), mate[j]) if not fresh else level_between(m, mate[j])
        biases = [[mask_bias(level, 2 * c + h, 2 * c + t) for h in range(2)] for t in range(2)]
        return pair(*frame(qg, stat, s), biases, j, fresh)

    def window(side):
        for copy in win[side]:
            copy.wait_recv()

        biases = [
            [mask_bias(0, 2 * beside[side] + h, 2 * c + t) for h in range(2)] for t in range(2)
        ]
        wdq_out[side] = pair(*frame(wqg, wstat, side), biases, 0).astype(BF16)
        wret[side].start()

    def visit_all(s):
        q, g, lse, delta = frame(qg, stat, s)
        keys = jnp.concatenate([kv[j, 0] for j in range(4)], axis=0)
        values = jnp.concatenate([kv[j, 1] for j in range(4)], axis=0)
        scores = dot_nt(keys, q)
        dprobs = dot_nt(values, g)
        probs, dscores = [], []
        for j in range(4):
            level = level_between(source(s), mate[j])
            for t in range(2):
                bias = [mask_bias(level, 2 * c + h, 2 * c + t) for h in range(2)]
                shift = lse + jnp.where(lane < TILE, bias[0], bias[1])
                at = (2 * j + t) * TILE
                prob = jnp.exp2(scores[at : at + TILE] * (scale * LOG2E) - shift)
                probs.append(prob.astype(BF16))
                dscores.append((prob * (dprobs[at : at + TILE] - delta)).astype(BF16))
        prob = jnp.concatenate(probs, axis=0)
        dscore = jnp.concatenate(dscores, axis=0)
        dv = dot_nn(prob, g)
        dk = dot_nn(dscore, q)
        for j in range(4):
            dv_acc[j] += dv[j * ROWS : (j + 1) * ROWS]
            dk_acc[j] += dk[j * ROWS : (j + 1) * ROWS]
        kt_all = jnp.concatenate([kt[j] for j in range(4)], axis=1)
        return dot_nn(kt_all, dscore)

    even = jnp.logical_not(odd)
    far_left = even & has[0] & (c % (space_count // 2) == 0)

    def answer(side):
        pl.semaphore_wait(in_sem.at[side], 1)
        win_start(1 - side)

    key_t(0)
    dq_acc[...] = visit(0, 0, True)

    @pl.when(even & has[0] & (c % (space_count // 2) != 0))
    def _():
        answer(0)

    for copy in kv1:
        copy.wait_recv()
    key_t(1)
    dq_acc[...] += visit(0, 1, True)
    arrive((1, 2))

    @pl.when(even & has[1])
    def _():
        answer(1)

    for copy in kv2:
        copy.wait_recv()
    kv3.start()
    key_t(2)
    dq_acc[...] += visit(0, 2, True)
    kv3.wait_recv()
    key_t(3)
    dq_acc[...] += visit(0, 3, True)

    def turn(turn_index, carry):
        s = turn_index
        @pl.when(s == 2)
        def _():
            arrive((3, 4))

        @pl.when((s == 4) & far_left)
        def _():
            answer(0)

        @pl.when(has[0] & (s == jnp.where(c % (space_count // 2) == 0, 6, 4)))
        def _():
            window(0)

        @pl.when(has[1] & (s == 5))
        def _():
            window(1)

        for n in (5, 6, 7):
            @pl.when(s == n)
            def _():
                arrive((n,))

        total = visit_all(s)
        middle = (s == 3) | (s == 4)

        @pl.when(middle)
        def _():
            dq_mid[s - 3] = total

        @pl.when(s == 7)
        def _():
            for tile in range(2):
                dq7_out[tile] = total[:, tile * TILE : (tile + 1) * TILE].astype(BF16)
                ret7(tile).start()

        @pl.when(jnp.logical_not(middle | (s == 7)))
        def _():
            dq_out[s] = total.astype(BF16)
            ret(s).start()

        return carry

    lax.fori_loop(1, STEPS, turn, 0)

    sums = (dk_acc, dv_acc)

    def give(j, extra=None):
        for n in range(2):
            part = sums[n][j]
            if extra is not None:
                kvret[extra, n].wait_recv()
                part = part + kv_in[extra, n].astype(F32)
            kv_out[j, n] = part.astype(BF16)
            kvret[j, n].start()

    give(3)
    give(1)
    give(2, 3)

    for n in range(2):
        ret(jnp.int32(5 + n)).wait_recv()
        part = dq_mid[n] + dq_in[5 + n].astype(F32)
        ret7(n).wait_recv()
        far_part = dq7_in[n].astype(F32)
        halves = [part[:, :TILE], part[:, TILE:]]
        halves[n] = halves[n] + far_part
        for tile in range(2):
            dq_out[3 + n, :, tile * TILE : (tile + 1) * TILE] = halves[tile].astype(BF16)
        ret(jnp.int32(3 + n), 2).start()

    for side in range(2):
        @pl.when(has[1 - side])
        def _():
            wret[side].wait_recv()
            dq_acc[...] += wdq_in[side].astype(F32)
    total = dq_acc[...]
    for step in range(1, 5):
        ret(jnp.int32(step), (step + 1) // 2).wait_recv()
        total = total + dq_in[step].astype(F32)
    out_ref[:ROWS, :] = (total.T * scale).astype(BF16)

    for n in range(2):
        part = sums[n][0]
        for slot in (1, 2):
            kvret[slot, n].wait_recv()
            part = part + kv_in[slot, n].astype(F32)
        out_ref[(n + 1) * ROWS : (n + 2) * ROWS, :] = (part * scale if n == 0 else part).astype(BF16)

    for step in range(1, STEPS):
        for copy in hop[step].values():
            copy.wait_send()
        if step < 7:
            ret(jnp.int32(step), 2 if step in (3, 4) else 1).wait_send()
    for tile in range(2):
        ret7(tile).wait_send()
    for copy in kv1 + kv2 + [kv3] + list(kvret.values()):
        copy.wait_send()
    for side in range(2):
        @pl.when(has[side])
        def _():
            for copy in win[1 - side]:
                copy.wait_send()
            wret[side].wait_send()


def body(slab_count, space_count, query, key, value, out_saved, grad_out, log_norm, band, frames):
    any_spec = pl.BlockSpec(memory_space=pl.ANY)
    smem = pl.BlockSpec(memory_space=pltpu.SMEM)
    vmem = pl.BlockSpec(memory_space=pltpu.VMEM)
    dma = pltpu.SemaphoreType.DMA
    grads = pl.pallas_call(
        functools.partial(kernel, slab_count, space_count, band.shape[0]),
        out_shape=jax.ShapeDtypeStruct((3 * ROWS, DIM), BF16),
        in_specs=[any_spec] * 5 + [vmem, smem, smem],
        out_specs=vmem,
        scratch_shapes=[
            pltpu.VMEM((8, 2, ROWS, DIM), BF16),
            pltpu.VMEM((8, 2, 2, TILE), F32),
            pltpu.VMEM((2, 2, ROWS, DIM), BF16),
            pltpu.VMEM((2, 2, 2, TILE), F32),
            pltpu.VMEM((4, 2, ROWS, DIM), BF16),
            pltpu.VMEM((4, DIM, ROWS), BF16),
            pltpu.VMEM((ROWS, DIM), BF16),
            pltpu.VMEM((4, ROWS, DIM), F32),
            pltpu.VMEM((4, ROWS, DIM), F32),
            pltpu.VMEM((DIM, ROWS), F32),
            pltpu.VMEM((8, DIM, ROWS), BF16),
            pltpu.VMEM((8, DIM, ROWS), BF16),
            pltpu.VMEM((2, DIM, ROWS), F32),
            pltpu.VMEM((2, DIM, TILE), BF16),
            pltpu.VMEM((2, DIM, TILE), BF16),
            pltpu.VMEM((2, DIM, ROWS), BF16),
            pltpu.VMEM((2, DIM, ROWS), BF16),
            pltpu.VMEM((4, 2, ROWS, DIM), BF16),
            pltpu.VMEM((4, 2, ROWS, DIM), BF16),
            dma((8,)),
            dma((8, 2, 3)),
            dma((8, 2, 3)),
            dma((2, 3)),
            dma((2, 3)),
            dma((5,)),
            dma((5,)),
            dma((9,)),
            dma((9,)),
            dma((2,)),
            dma((2,)),
            dma((4, 2)),
            dma((4, 2)),
            pltpu.SemaphoreType.REGULAR((2,)),
        ],
        compiler_params=pltpu.CompilerParams(
            collective_id=0, has_side_effects=True, vmem_limit_bytes=24 * 1024 * 1024
        ),
    )(*[pltpu.with_memory_space_constraint(a, pltpu.HBM) for a in (query, key, value, out_saved, grad_out, log_norm, band, frames)])

    return tuple(grads[n * ROWS : (n + 1) * ROWS] for n in range(3))


def solution(mesh):
    rows = P(("slab", "space"), None)
    return jax.shard_map(
        functools.partial(body, mesh.shape["slab"], mesh.shape["space"]),
        mesh=mesh,
        in_specs=(rows, rows, rows, rows, rows, P(None, ("slab", "space")), P(), P()),
        out_specs=(rows, rows, rows),
        check_vma=False,
    )
```

```python
import functools
import math

import jax
import jax.numpy as jnp
from jax import lax
from jax.experimental import pallas as pl
from jax.experimental.pallas import tpu as pltpu
from jax.sharding import PartitionSpec as P

MESH = pl.DeviceIdType.MESH
TILE = 128
ROWS = 256
DIM = 128
LOG2E = math.log2(math.e)
MASKED = 1e30
BF16 = jnp.bfloat16
F32 = jnp.float32

ONWARD = {1: 3, 2: 4, 3: 5, 4: 6}
STEPS = 8


def dot_nt(a, b):
    return lax.dot_general(a, b, (((1,), (1,)), ((), ())), preferred_element_type=F32)


def dot_nn(a, b):
    return lax.dot_general(a, b, (((1,), (0,)), ((), ())), preferred_element_type=F32)


def kernel(
    slab_count,
    space_count,
    level_count,
    q_hbm,
    k_hbm,
    v_hbm,
    o_hbm,
    g_hbm,
    lse_ref,
    band,
    frames,
    out_ref,
    qg,
    stat,
    wqg,
    wstat,
    kv,
    kt,
    o_buf,
    dk_acc,
    dv_acc,
    dq_acc,
    dq_out,
    dq_in,
    dq_mid,
    dq7_out,
    dq7_in,
    wdq_out,
    wdq_in,
    kv_out,
    kv_in,
    local_sem,
    fwd_send,
    fwd_recv,
    win_send,
    win_recv,
    kv_send,
    kv_recv,
    ret_send,
    ret_recv,
    wret_send,
    wret_recv,
    kvret_send,
    kvret_recv,
    in_sem,
):
    m = lax.axis_index("slab")
    c = lax.axis_index("space")
    group = m % 4
    base = m - group
    core = group % 2
    x_lo = group // 2
    mate = [
        m,
        base + 2 * x_lo + (1 - core),
        base + 2 * (1 - x_lo) + core,
        base + 2 * (1 - x_lo) + (1 - core),
    ]
    scale = DIM ** (-0.5)
    has = [c > 0, c < space_count - 1]
    beside = [jnp.maximum(c - 1, 0), jnp.minimum(c + 1, space_count - 1)]
    odd = c % 2 == 1

    def ring(hops):
        return (m + 4 * hops + slab_count) % slab_count

    up, down = ring(1), ring(-1)

    barrier = pltpu.get_barrier_semaphore()
    for peer in (up, down, mate[2], mate[1]):
        pl.semaphore_signal(barrier, inc=1, device_id={"slab": peer}, device_id_type=MESH)
    for side in range(2):
        @pl.when(has[side] & jnp.logical_not(odd))
        def _():
            pl.semaphore_signal(
                barrier, inc=1, device_id={"space": beside[side]}, device_id_type=MESH
            )

    loads = [
        pltpu.make_async_copy(src, dst, local_sem.at[n])
        for n, (src, dst) in enumerate(
            (
                (g_hbm, qg.at[0, 1]),
                (o_hbm, o_buf),
                (k_hbm, kv.at[0, 0]),
                (q_hbm, qg.at[0, 0]),
                (v_hbm, kv.at[0, 1]),
            )
        )
    ]
    for copy in loads:
        copy.start()

    def remote(src, dst, sems, index, peer):
        return pltpu.make_async_remote_copy(
            src_ref=src,
            dst_ref=dst,
            send_sem=sems[0].at[index],
            recv_sem=sems[1].at[index],
            device_id=peer,
            device_id_type=MESH,
        )

    fwd, kvs, wins = (fwd_send, fwd_recv), (kv_send, kv_recv), (win_send, win_recv)
    own = (q_hbm, g_hbm)

    def frame_copies(src, dst, peer, tiles=(0, 1)):
        out = {}
        for tile in tiles:
            rows = pl.ds(tile * TILE, TILE)
            for part in range(2):
                source_ref = own[part].at[rows] if src == 0 else qg.at[src, part, rows]
                out[tile, part] = remote(
                    source_ref, qg.at[dst, part, rows], fwd, (dst, tile, part), {"slab": peer}
                )
            out[tile, 2] = remote(
                stat.at[src, tile], stat.at[dst, tile], fwd, (dst, tile, 2), {"slab": peer}
            )
        return out

    hop = {}
    for s in range(1, 7):
        hop[s] = frame_copies(max(s - 2, 0), s, up if s % 2 else down)
    far = {0: frame_copies(3, 7, ring(2), (0,)), 1: frame_copies(4, 7, ring(-2), (1,))}
    hop[7] = {**far[0], **far[1]}

    def arrive(steps, numbers=range(6)):
        keys = {1: ((0, 0), (0, 1), (0, 2), (1, 0), (1, 1), (1, 2))}
        keys[0] = keys[1][3:] + keys[1][:3]
        for n in numbers:
            pieces = [(step, keys[step % 2][n]) for step in steps]
            for step, key in pieces:
                hop[step][key].wait_recv()
                if step in ONWARD and (step not in (3, 4) or n >= 3):
                    hop[ONWARD[step]][key].start()
            if steps == (3, 4) and n < 3:
                for _, key in pieces:
                    hop[7][key].start()
                for step, key in pieces:
                    hop[ONWARD[step]][key].start()

    kv1 = [remote(h, kv.at[1, n], kvs, n, {"slab": mate[1]}) for n, h in enumerate((k_hbm, v_hbm))]
    kv2 = [
        remote(h, kv.at[2, n], kvs, 2 + n, {"slab": mate[2]}) for n, h in enumerate((k_hbm, v_hbm))
    ]
    kv3 = remote(kv.at[2], kv.at[3], kvs, 4, {"slab": mate[1]})

    win = [
        [
            remote(q_hbm, wqg.at[side, 0], wins, (side, 0), {"space": beside[1 - side]}),
            remote(g_hbm, wqg.at[side, 1], wins, (side, 1), {"space": beside[1 - side]}),
            remote(stat.at[0], wstat.at[side], wins, (side, 2), {"space": beside[1 - side]}),
        ]
        for side in range(2)
    ]
    wret = [
        remote(
            wdq_out.at[side], wdq_in.at[side], (wret_send, wret_recv), side, {"space": beside[side]}
        )
        for side in range(2)
    ]

    def source(step):
        return ring(jnp.where(step % 2 == 1, -1, 1) * ((step + 1) // 2))

    rets = (ret_send, ret_recv)

    def side_of(step):
        return jnp.where(step % 2 == 1, -1, 1)

    def ret(step, hops=1):
        return remote(
            dq_out.at[step], dq_in.at[step], rets, step, {"slab": ring(side_of(step) * hops)}
        )

    def ret7(tile):
        return remote(
            dq7_out.at[tile], dq7_in.at[tile], rets, 7 + tile, {"slab": ring(-2 if tile == 0 else 2)}
        )

    kvret = {
        (slot, n): remote(
            kv_out.at[slot, n],
            kv_in.at[slot, n],
            (kvret_send, kvret_recv),
            (slot, n),
            {"slab": mate[peer]},
        )
        for slot, peer in ((1, 1), (2, 2), (3, 1))
        for n in range(2)
    }

    pl.semaphore_wait(
        barrier, 4 + jnp.where(odd, has[0].astype(jnp.int32) + has[1].astype(jnp.int32), 0)
    )

    for side in range(2):
        @pl.when(odd & has[side])
        def _():
            pl.semaphore_signal(
                in_sem.at[1 - side],
                inc=1,
                device_id={"space": beside[side]},
                device_id_type=MESH,
            )

    for key in ((0, 0), (0, 1), (1, 0), (1, 1)):
        hop[1][key].start()
        hop[2][key].start()
    for copy in kv2 + kv1:
        copy.start()

    for copy in loads[:2]:
        copy.wait()
    for t in range(2):
        rows = pl.ds(t * TILE, TILE)
        product = qg[0, 1, rows, :].astype(F32) * o_buf[rows, :].astype(F32)
        stat[0, t, 1:2, :] = jnp.sum(product.T, axis=0, keepdims=True)
        stat[0, t, 0:1, :] = lse_ref[:, t * TILE : (t + 1) * TILE] * LOG2E
    for tile in range(2):
        hop[1][tile, 2].start()
        hop[2][tile, 2].start()

    def win_start(side):
        for copy in win[side]:
            copy.start()

    for side in range(2):
        @pl.when(odd & has[1 - side])
        def _():
            win_start(side)

    for copy in loads[2:]:
        copy.wait()

    lane = lax.broadcasted_iota(jnp.int32, (1, ROWS), 1)

    def mask_bias(level, q_tile, k_tile):
        return jnp.where(band[level, q_tile, k_tile] > 0, 0.0, MASKED).astype(F32)

    def level_between(a, b):
        distance = jnp.abs(frames[a] - frames[b])
        level = jnp.int32(0)
        for n in range(level_count - 1):
            level = level + jnp.where(distance >= 2**n, 1, 0)
        return level

    def key_t(j):
        kt[j] = kv[j, 0].astype(F32).T.astype(BF16)

    def pair(q, g, lse, delta, biases, j, fresh=False):
        key = kv[j, 0]
        shift = [lse + jnp.where(lane < TILE, biases[t][0], biases[t][1]) for t in range(2)]
        shifts = jnp.concatenate(
            [jnp.broadcast_to(shift[t], (TILE, ROWS)) for t in range(2)], axis=0
        )
        prob = jnp.exp2(dot_nt(key, q) * (scale * LOG2E) - shifts)
        dprob = dot_nt(kv[j, 1], g)
        dscore = (prob * (dprob - delta)).astype(BF16)
        dv = dot_nn(prob.astype(BF16), g)
        dk = dot_nn(dscore, q)
        dv_acc[j] = dv if fresh else dv_acc[j] + dv
        dk_acc[j] = dk if fresh else dk_acc[j] + dk
        return dot_nn(kt[j], dscore)

    def frame(block, rows, s):
        return [block[s, 0], block[s, 1]] + [
            jnp.concatenate([rows[s, 0, n : n + 1, :], rows[s, 1, n : n + 1, :]], axis=1)
            for n in range(2)
        ]

    def visit(s, j, fresh=False):
        level = level_between(source(s), mate[j]) if not fresh else level_between(m, mate[j])
        biases = [[mask_bias(level, 2 * c + h, 2 * c + t) for h in range(2)] for t in range(2)]
        return pair(*frame(qg, stat, s), biases, j, fresh)

    def window(side):
        for copy in win[side]:
            copy.wait_recv()

        biases = [
            [mask_bias(0, 2 * beside[side] + h, 2 * c + t) for h in range(2)] for t in range(2)
        ]
        wdq_out[side] = pair(*frame(wqg, wstat, side), biases, 0).astype(BF16)
        wret[side].start()

    def visit_all(s):
        q, g, lse, delta = frame(qg, stat, s)
        keys = jnp.concatenate([kv[j, 0] for j in range(4)], axis=0)
        values = jnp.concatenate([kv[j, 1] for j in range(4)], axis=0)
        scores = dot_nt(keys, q)
        dprobs = dot_nt(values, g)
        probs, dscores = [], []
        for j in range(4):
            level = level_between(source(s), mate[j])
            for t in range(2):
                bias = [mask_bias(level, 2 * c + h, 2 * c + t) for h in range(2)]
                shift = lse + jnp.where(lane < TILE, bias[0], bias[1])
                at = (2 * j + t) * TILE
                prob = jnp.exp2(scores[at : at + TILE] * (scale * LOG2E) - shift)
                probs.append(prob.astype(BF16))
                dscores.append((prob * (dprobs[at : at + TILE] - delta)).astype(BF16))
        prob = jnp.concatenate(probs, axis=0)
        dscore = jnp.concatenate(dscores, axis=0)
        dv = dot_nn(prob, g)
        dk = dot_nn(dscore, q)
        for j in range(4):
            dv_acc[j] += dv[j * ROWS : (j + 1) * ROWS]
            dk_acc[j] += dk[j * ROWS : (j + 1) * ROWS]
        kt_all = jnp.concatenate([kt[j] for j in range(4)], axis=1)
        return dot_nn(kt_all, dscore)

    even = jnp.logical_not(odd)
    far_left = even & has[0] & (c % (space_count // 2) == 0)

    def answer(side):
        pl.semaphore_wait(in_sem.at[side], 1)
        win_start(1 - side)

    key_t(0)
    dq_acc[...] = visit(0, 0, True)

    @pl.when(even & has[0] & (c % (space_count // 2) != 0))
    def _():
        answer(0)

    for copy in kv1:
        copy.wait_recv()
    key_t(1)
    dq_acc[...] += visit(0, 1, True)
    arrive((1, 2))

    @pl.when(even & has[1])
    def _():
        answer(1)

    for copy in kv2:
        copy.wait_recv()
    kv3.start()
    key_t(2)
    dq_acc[...] += visit(0, 2, True)
    kv3.wait_recv()
    key_t(3)
    dq_acc[...] += visit(0, 3, True)

    def turn(turn_index, carry):
        s = jnp.where(turn_index < 5, turn_index, 5 + (turn_index - 3) % 3)
        for n in (1, 2):
            @pl.when(s == n)
            def _():
                arrive((3, 4), range(3 * n - 3, 3 * n))

        @pl.when((s == 4) & far_left)
        def _():
            answer(0)

        @pl.when(has[0] & (s == jnp.where(c % (space_count // 2) == 0, 6, 4)))
        def _():
            window(0)

        @pl.when(has[1] & (s == 5))
        def _():
            window(1)

        for n in (5, 6, 7):
            @pl.when(s == n)
            def _():
                arrive((n,))

        total = visit_all(s)
        middle = (s == 3) | (s == 4)

        @pl.when(middle)
        def _():
            dq_mid[s - 3] = total

        @pl.when(s == 7)
        def _():
            for tile in range(2):
                dq7_out[tile] = total[:, tile * TILE : (tile + 1) * TILE].astype(BF16)
                ret7(tile).start()

        @pl.when(jnp.logical_not(middle | (s == 7)))
        def _():
            dq_out[s] = total.astype(BF16)
            ret(s).start()

        return carry

    lax.fori_loop(1, STEPS, turn, 0)

    sums = (dk_acc, dv_acc)

    def give(j, extra=None):
        for n in range(2):
            part = sums[n][j]
            if extra is not None:
                kvret[extra, n].wait_recv()
                part = part + kv_in[extra, n].astype(F32)
            kv_out[j, n] = part.astype(BF16)
            kvret[j, n].start()

    give(3)
    give(1)
    give(2, 3)

    for n in range(2):
        ret(jnp.int32(5 + n)).wait_recv()
        part = dq_mid[n] + dq_in[5 + n].astype(F32)
        ret7(n).wait_recv()
        far_part = dq7_in[n].astype(F32)
        halves = [part[:, :TILE], part[:, TILE:]]
        halves[n] = halves[n] + far_part
        for tile in range(2):
            dq_out[3 + n, :, tile * TILE : (tile + 1) * TILE] = halves[tile].astype(BF16)
        ret(jnp.int32(3 + n), 2).start()

    for side in range(2):
        @pl.when(has[1 - side])
        def _():
            wret[side].wait_recv()
            dq_acc[...] += wdq_in[side].astype(F32)
    total = dq_acc[...]
    for step in range(1, 5):
        ret(jnp.int32(step), (step + 1) // 2).wait_recv()
        total = total + dq_in[step].astype(F32)
    out_ref[:ROWS, :] = (total.T * scale).astype(BF16)

    for n in range(2):
        part = sums[n][0]
        for slot in (1, 2):
            kvret[slot, n].wait_recv()
            part = part + kv_in[slot, n].astype(F32)
        out_ref[(n + 1) * ROWS : (n + 2) * ROWS, :] = (part * scale if n == 0 else part).astype(BF16)

    for step in range(1, STEPS):
        for copy in hop[step].values():
            copy.wait_send()
        if step < 7:
            ret(jnp.int32(step), 2 if step in (3, 4) else 1).wait_send()
    for tile in range(2):
        ret7(tile).wait_send()
    for copy in kv1 + kv2 + [kv3] + list(kvret.values()):
        copy.wait_send()
    for side in range(2):
        @pl.when(has[side])
        def _():
            for copy in win[1 - side]:
                copy.wait_send()
            wret[side].wait_send()


def body(slab_count, space_count, query, key, value, out_saved, grad_out, log_norm, band, frames):
    any_spec = pl.BlockSpec(memory_space=pl.ANY)
    smem = pl.BlockSpec(memory_space=pltpu.SMEM)
    vmem = pl.BlockSpec(memory_space=pltpu.VMEM)
    dma = pltpu.SemaphoreType.DMA
    grads = pl.pallas_call(
        functools.partial(kernel, slab_count, space_count, band.shape[0]),
        out_shape=jax.ShapeDtypeStruct((3 * ROWS, DIM), BF16),
        in_specs=[any_spec] * 5 + [vmem, smem, smem],
        out_specs=vmem,
        scratch_shapes=[
            pltpu.VMEM((8, 2, ROWS, DIM), BF16),
            pltpu.VMEM((8, 2, 2, TILE), F32),
            pltpu.VMEM((2, 2, ROWS, DIM), BF16),
            pltpu.VMEM((2, 2, 2, TILE), F32),
            pltpu.VMEM((4, 2, ROWS, DIM), BF16),
            pltpu.VMEM((4, DIM, ROWS), BF16),
            pltpu.VMEM((ROWS, DIM), BF16),
            pltpu.VMEM((4, ROWS, DIM), F32),
            pltpu.VMEM((4, ROWS, DIM), F32),
            pltpu.VMEM((DIM, ROWS), F32),
            pltpu.VMEM((8, DIM, ROWS), BF16),
            pltpu.VMEM((8, DIM, ROWS), BF16),
            pltpu.VMEM((2, DIM, ROWS), F32),
            pltpu.VMEM((2, DIM, TILE), BF16),
            pltpu.VMEM((2, DIM, TILE), BF16),
            pltpu.VMEM((2, DIM, ROWS), BF16),
            pltpu.VMEM((2, DIM, ROWS), BF16),
            pltpu.VMEM((4, 2, ROWS, DIM), BF16),
            pltpu.VMEM((4, 2, ROWS, DIM), BF16),
            dma((8,)),
            dma((8, 2, 3)),
            dma((8, 2, 3)),
            dma((2, 3)),
            dma((2, 3)),
            dma((5,)),
            dma((5,)),
            dma((9,)),
            dma((9,)),
            dma((2,)),
            dma((2,)),
            dma((4, 2)),
            dma((4, 2)),
            pltpu.SemaphoreType.REGULAR((2,)),
        ],
        compiler_params=pltpu.CompilerParams(
            collective_id=0, has_side_effects=True, vmem_limit_bytes=24 * 1024 * 1024
        ),
    )(*[pltpu.with_memory_space_constraint(a, pltpu.HBM) for a in (query, key, value, out_saved, grad_out, log_norm, band, frames)])

    return tuple(grads[n * ROWS : (n + 1) * ROWS] for n in range(3))


def solution(mesh):
    rows = P(("slab", "space"), None)
    return jax.shard_map(
        functools.partial(body, mesh.shape["slab"], mesh.shape["space"]),
        mesh=mesh,
        in_specs=(rows, rows, rows, rows, rows, P(None, ("slab", "space")), P(), P()),
        out_specs=(rows, rows, rows),
        check_vma=False,
    )
```

```python
import functools
import math

import jax
import jax.numpy as jnp
from jax import lax
from jax.experimental import pallas as pl
from jax.experimental.pallas import tpu as pltpu
from jax.sharding import PartitionSpec as P

MESH = pl.DeviceIdType.MESH
TILE = 128
ROWS = 256
DIM = 128
LOG2E = math.log2(math.e)
MASKED = 1e30
BF16 = jnp.bfloat16
F32 = jnp.float32

ONWARD = {1: 3, 2: 4, 3: 5, 4: 6}
STEPS = 8


def dot_nt(a, b):
    return lax.dot_general(a, b, (((1,), (1,)), ((), ())), preferred_element_type=F32)


def dot_nn(a, b):
    return lax.dot_general(a, b, (((1,), (0,)), ((), ())), preferred_element_type=F32)


def kernel(
    slab_count,
    space_count,
    level_count,
    q_hbm,
    k_hbm,
    v_hbm,
    o_hbm,
    g_hbm,
    lse_ref,
    band,
    frames,
    out_ref,
    qg,
    stat,
    wqg,
    wstat,
    kv,
    kt,
    o_buf,
    dk_acc,
    dv_acc,
    dq_acc,
    dq_out,
    dq_in,
    dq_mid,
    dq7_out,
    dq7_in,
    wdq_out,
    wdq_in,
    kv_out,
    kv_in,
    local_sem,
    fwd_send,
    fwd_recv,
    win_send,
    win_recv,
    kv_send,
    kv_recv,
    ret_send,
    ret_recv,
    wret_send,
    wret_recv,
    kvret_send,
    kvret_recv,
    in_sem,
):
    m = lax.axis_index("slab")
    c = lax.axis_index("space")
    group = m % 4
    base = m - group
    core = group % 2
    x_lo = group // 2
    mate = [
        m,
        base + 2 * x_lo + (1 - core),
        base + 2 * (1 - x_lo) + core,
        base + 2 * (1 - x_lo) + (1 - core),
    ]
    scale = DIM ** (-0.5)
    has = [c > 0, c < space_count - 1]
    beside = [jnp.maximum(c - 1, 0), jnp.minimum(c + 1, space_count - 1)]
    odd = c % 2 == 1

    def ring(hops):
        return (m + 4 * hops + slab_count) % slab_count

    up, down = ring(1), ring(-1)

    barrier = pltpu.get_barrier_semaphore()
    for peer in (up, down, mate[2], mate[1]):
        pl.semaphore_signal(barrier, inc=1, device_id={"slab": peer}, device_id_type=MESH)
    for side in range(2):
        @pl.when(has[side] & jnp.logical_not(odd))
        def _():
            pl.semaphore_signal(
                barrier, inc=1, device_id={"space": beside[side]}, device_id_type=MESH
            )

    loads = [
        pltpu.make_async_copy(src, dst, local_sem.at[n])
        for n, (src, dst) in enumerate(
            (
                (g_hbm, qg.at[0, 1]),
                (o_hbm, o_buf),
                (k_hbm, kv.at[0, 0]),
                (q_hbm, qg.at[0, 0]),
                (v_hbm, kv.at[0, 1]),
            )
        )
    ]
    for copy in loads:
        copy.start()

    def remote(src, dst, sems, index, peer):
        return pltpu.make_async_remote_copy(
            src_ref=src,
            dst_ref=dst,
            send_sem=sems[0].at[index],
            recv_sem=sems[1].at[index],
            device_id=peer,
            device_id_type=MESH,
        )

    fwd, kvs, wins = (fwd_send, fwd_recv), (kv_send, kv_recv), (win_send, win_recv)
    own = (q_hbm, g_hbm)

    def frame_copies(src, dst, peer, tiles=(0, 1)):
        out = {}
        for tile in tiles:
            rows = pl.ds(tile * TILE, TILE)
            for part in range(2):
                source_ref = own[part].at[rows] if src == 0 else qg.at[src, part, rows]
                out[tile, part] = remote(
                    source_ref, qg.at[dst, part, rows], fwd, (dst, tile, part), {"slab": peer}
                )
            out[tile, 2] = remote(
                stat.at[src, tile], stat.at[dst, tile], fwd, (dst, tile, 2), {"slab": peer}
            )
        return out

    hop = {}
    for s in range(1, 7):
        hop[s] = frame_copies(max(s - 2, 0), s, up if s % 2 else down)
    far = {0: frame_copies(3, 7, ring(2), (0,)), 1: frame_copies(4, 7, ring(-2), (1,))}
    hop[7] = {**far[0], **far[1]}

    def arrive(steps):
        keys = {1: ((0, 0), (0, 1), (0, 2), (1, 0), (1, 1), (1, 2))}
        keys[0] = keys[1][3:] + keys[1][:3]
        for n in range(6):
            pieces = [(step, keys[step % 2][n]) for step in steps]
            for step, key in pieces:
                hop[step][key].wait_recv()
                if step in ONWARD and (step not in (3, 4) or n >= 3):
                    hop[ONWARD[step]][key].start()
            if steps == (3, 4) and n < 3:
                for _, key in pieces:
                    hop[7][key].start()
                for step, key in pieces:
                    hop[ONWARD[step]][key].start()

    kv1 = [remote(h, kv.at[1, n], kvs, n, {"slab": mate[1]}) for n, h in enumerate((k_hbm, v_hbm))]
    kv2 = [
        remote(h, kv.at[2, n], kvs, 2 + n, {"slab": mate[2]}) for n, h in enumerate((k_hbm, v_hbm))
    ]
    kv3 = remote(kv.at[2], kv.at[3], kvs, 4, {"slab": mate[1]})

    win = [
        [
            remote(q_hbm, wqg.at[side, 0], wins, (side, 0), {"space": beside[1 - side]}),
            remote(g_hbm, wqg.at[side, 1], wins, (side, 1), {"space": beside[1 - side]}),
            remote(stat.at[0], wstat.at[side], wins, (side, 2), {"space": beside[1 - side]}),
        ]
        for side in range(2)
    ]
    wret = [
        remote(
            wdq_out.at[side], wdq_in.at[side], (wret_send, wret_recv), side, {"space": beside[side]}
        )
        for side in range(2)
    ]

    def source(step):
        return ring(jnp.where(step % 2 == 1, -1, 1) * ((step + 1) // 2))

    rets = (ret_send, ret_recv)

    def side_of(step):
        return jnp.where(step % 2 == 1, -1, 1)

    def ret(step, hops=1):
        return remote(
            dq_out.at[step], dq_in.at[step], rets, step, {"slab": ring(side_of(step) * hops)}
        )

    def ret7(tile):
        return remote(
            dq7_out.at[tile], dq7_in.at[tile], rets, 7 + tile, {"slab": ring(-2 if tile == 0 else 2)}
        )

    kvret = {
        (slot, n): remote(
            kv_out.at[slot, n],
            kv_in.at[slot, n],
            (kvret_send, kvret_recv),
            (slot, n),
            {"slab": mate[peer]},
        )
        for slot, peer in ((1, 1), (2, 2), (3, 1))
        for n in range(2)
    }

    pl.semaphore_wait(
        barrier, 4 + jnp.where(odd, has[0].astype(jnp.int32) + has[1].astype(jnp.int32), 0)
    )

    for side in range(2):
        @pl.when(odd & has[side])
        def _():
            pl.semaphore_signal(
                in_sem.at[1 - side],
                inc=1,
                device_id={"space": beside[side]},
                device_id_type=MESH,
            )

    for key in ((0, 0), (0, 1), (1, 0), (1, 1)):
        hop[1][key].start()
        hop[2][key].start()
    for copy in kv2 + kv1:
        copy.start()

    for copy in loads[:2]:
        copy.wait()
    for t in range(2):
        rows = pl.ds(t * TILE, TILE)
        product = qg[0, 1, rows, :].astype(F32) * o_buf[rows, :].astype(F32)
        stat[0, t, 1:2, :] = jnp.sum(product.T, axis=0, keepdims=True)
        stat[0, t, 0:1, :] = lse_ref[:, t * TILE : (t + 1) * TILE] * LOG2E
    for tile in range(2):
        hop[1][tile, 2].start()
        hop[2][tile, 2].start()

    def win_start(side):
        for copy in win[side]:
            copy.start()

    for side in range(2):
        @pl.when(odd & has[1 - side])
        def _():
            win_start(side)

    for copy in loads[2:]:
        copy.wait()

    lane = lax.broadcasted_iota(jnp.int32, (1, ROWS), 1)

    def mask_bias(level, q_tile, k_tile):
        return jnp.where(band[level, q_tile, k_tile] > 0, 0.0, MASKED).astype(F32)

    def level_between(a, b):
        distance = jnp.abs(frames[a] - frames[b])
        level = jnp.int32(0)
        for n in range(level_count - 1):
            level = level + jnp.where(distance >= 2**n, 1, 0)
        return level

    def key_t(j):
        kt[j] = kv[j, 0].astype(F32).T.astype(BF16)

    def pair(q, g, lse, delta, biases, j, fresh=False):
        key = kv[j, 0]
        shift = [lse + jnp.where(lane < TILE, biases[t][0], biases[t][1]) for t in range(2)]
        shifts = jnp.concatenate(
            [jnp.broadcast_to(shift[t], (TILE, ROWS)) for t in range(2)], axis=0
        )
        prob = jnp.exp2(dot_nt(key, q) * (scale * LOG2E) - shifts)
        dprob = dot_nt(kv[j, 1], g)
        dscore = (prob * (dprob - delta)).astype(BF16)
        dv = dot_nn(prob.astype(BF16), g)
        dk = dot_nn(dscore, q)
        dv_acc[j] = dv if fresh else dv_acc[j] + dv
        dk_acc[j] = dk if fresh else dk_acc[j] + dk
        return dot_nn(kt[j], dscore)

    def frame(block, rows, s):
        return [block[s, 0], block[s, 1]] + [
            jnp.concatenate([rows[s, 0, n : n + 1, :], rows[s, 1, n : n + 1, :]], axis=1)
            for n in range(2)
        ]

    def visit(s, j, fresh=False):
        level = level_between(source(s), mate[j]) if not fresh else level_between(m, mate[j])
        biases = [[mask_bias(level, 2 * c + h, 2 * c + t) for h in range(2)] for t in range(2)]
        return pair(*frame(qg, stat, s), biases, j, fresh)

    def window(side):
        for copy in win[side]:
            copy.wait_recv()

        biases = [
            [mask_bias(0, 2 * beside[side] + h, 2 * c + t) for h in range(2)] for t in range(2)
        ]
        wdq_out[side] = pair(*frame(wqg, wstat, side), biases, 0).astype(BF16)
        wret[side].start()

    def visit_all(s):
        q, g, lse, delta = frame(qg, stat, s)
        keys = jnp.concatenate([kv[j, 0] for j in range(4)], axis=0)
        values = jnp.concatenate([kv[j, 1] for j in range(4)], axis=0)
        scores = dot_nt(keys, q)
        dprobs = dot_nt(values, g)
        probs, dscores = [], []
        for j in range(4):
            level = level_between(source(s), mate[j])
            for t in range(2):
                bias = [mask_bias(level, 2 * c + h, 2 * c + t) for h in range(2)]
                shift = lse + jnp.where(lane < TILE, bias[0], bias[1])
                at = (2 * j + t) * TILE
                prob = jnp.exp2(scores[at : at + TILE] * (scale * LOG2E) - shift)
                probs.append(prob.astype(BF16))
                dscores.append((prob * (dprobs[at : at + TILE] - delta)).astype(BF16))
        prob = jnp.concatenate(probs, axis=0)
        dscore = jnp.concatenate(dscores, axis=0)
        dv = dot_nn(prob, g)
        dk = dot_nn(dscore, q)
        for j in range(4):
            dv_acc[j] += dv[j * ROWS : (j + 1) * ROWS]
            dk_acc[j] += dk[j * ROWS : (j + 1) * ROWS]
        kt_all = jnp.concatenate([kt[j] for j in range(4)], axis=1)
        return dot_nn(kt_all, dscore)

    even = jnp.logical_not(odd)
    far_left = even & has[0] & (c % (space_count // 2) == 0)

    def answer(side):
        pl.semaphore_wait(in_sem.at[side], 1)
        win_start(1 - side)

    key_t(0)
    dq_acc[...] = visit(0, 0, True)

    @pl.when(even & has[0] & (c % (space_count // 2) != 0))
    def _():
        answer(0)

    for copy in kv1:
        copy.wait_recv()
    key_t(1)
    dq_acc[...] += visit(0, 1, True)
    arrive((1, 2))

    @pl.when(even & has[1])
    def _():
        answer(1)

    for copy in kv2:
        copy.wait_recv()
    kv3.start()
    key_t(2)
    dq_acc[...] += visit(0, 2, True)
    kv3.wait_recv()
    key_t(3)
    dq_acc[...] += visit(0, 3, True)

    def turn(turn_index, carry):
        s = jnp.where(turn_index < 5, turn_index, 5 + (turn_index - 3) % 3)
        @pl.when(s == 1)
        def _():
            arrive((3, 4))

        @pl.when((s == 4) & far_left)
        def _():
            answer(0)

        @pl.when(has[0] & (s == jnp.where(c % (space_count // 2) == 0, 6, 4)))
        def _():
            window(0)

        @pl.when(has[1] & (s == 5))
        def _():
            window(1)

        for n in (5, 6, 7):
            @pl.when(s == n)
            def _():
                arrive((n,))

        total = visit_all(s)
        middle = (s == 3) | (s == 4)

        @pl.when(middle)
        def _():
            dq_mid[s - 3] = total

        @pl.when(s == 7)
        def _():
            for tile in range(2):
                dq7_out[tile] = total[:, tile * TILE : (tile + 1) * TILE].astype(BF16)
                ret7(tile).start()

        @pl.when(jnp.logical_not(middle | (s == 7)))
        def _():
            dq_out[s] = total.astype(BF16)
            ret(s).start()

        return carry

    lax.fori_loop(1, STEPS, turn, 0)

    sums = (dk_acc, dv_acc)

    def give(j, extra=None):
        for n in range(2):
            part = sums[n][j]
            if extra is not None:
                kvret[extra, n].wait_recv()
                part = part + kv_in[extra, n].astype(F32)
            kv_out[j, n] = part.astype(BF16)
            kvret[j, n].start()

    give(3)
    give(1)
    give(2, 3)

    for n in range(2):
        ret(jnp.int32(5 + n)).wait_recv()
        part = dq_mid[n] + dq_in[5 + n].astype(F32)
        ret7(n).wait_recv()
        far_part = dq7_in[n].astype(F32)
        halves = [part[:, :TILE], part[:, TILE:]]
        halves[n] = halves[n] + far_part
        for tile in range(2):
            dq_out[3 + n, :, tile * TILE : (tile + 1) * TILE] = halves[tile].astype(BF16)
        ret(jnp.int32(3 + n), 2).start()

    for side in range(2):
        @pl.when(has[1 - side])
        def _():
            wret[side].wait_recv()
            dq_acc[...] += wdq_in[side].astype(F32)
    total = dq_acc[...]
    for step in range(1, 5):
        ret(jnp.int32(step), (step + 1) // 2).wait_recv()
        total = total + dq_in[step].astype(F32)
    out_ref[:ROWS, :] = (total.T * scale).astype(BF16)

    for n in range(2):
        part = sums[n][0]
        for slot in (1, 2):
            kvret[slot, n].wait_recv()
            part = part + kv_in[slot, n].astype(F32)
        out_ref[(n + 1) * ROWS : (n + 2) * ROWS, :] = (part * scale if n == 0 else part).astype(BF16)

    for step in range(1, STEPS):
        for copy in hop[step].values():
            copy.wait_send()
        if step < 7:
            ret(jnp.int32(step), 2 if step in (3, 4) else 1).wait_send()
    for tile in range(2):
        ret7(tile).wait_send()
    for copy in kv1 + kv2 + [kv3] + list(kvret.values()):
        copy.wait_send()
    for side in range(2):
        @pl.when(has[side])
        def _():
            for copy in win[1 - side]:
                copy.wait_send()
            wret[side].wait_send()


def body(slab_count, space_count, query, key, value, out_saved, grad_out, log_norm, band, frames):
    any_spec = pl.BlockSpec(memory_space=pl.ANY)
    smem = pl.BlockSpec(memory_space=pltpu.SMEM)
    vmem = pl.BlockSpec(memory_space=pltpu.VMEM)
    dma = pltpu.SemaphoreType.DMA
    grads = pl.pallas_call(
        functools.partial(kernel, slab_count, space_count, band.shape[0]),
        out_shape=jax.ShapeDtypeStruct((3 * ROWS, DIM), BF16),
        in_specs=[any_spec] * 5 + [vmem, smem, smem],
        out_specs=vmem,
        scratch_shapes=[
            pltpu.VMEM((8, 2, ROWS, DIM), BF16),
            pltpu.VMEM((8, 2, 2, TILE), F32),
            pltpu.VMEM((2, 2, ROWS, DIM), BF16),
            pltpu.VMEM((2, 2, 2, TILE), F32),
            pltpu.VMEM((4, 2, ROWS, DIM), BF16),
            pltpu.VMEM((4, DIM, ROWS), BF16),
            pltpu.VMEM((ROWS, DIM), BF16),
            pltpu.VMEM((4, ROWS, DIM), F32),
            pltpu.VMEM((4, ROWS, DIM), F32),
            pltpu.VMEM((DIM, ROWS), F32),
            pltpu.VMEM((8, DIM, ROWS), BF16),
            pltpu.VMEM((8, DIM, ROWS), BF16),
            pltpu.VMEM((2, DIM, ROWS), F32),
            pltpu.VMEM((2, DIM, TILE), BF16),
            pltpu.VMEM((2, DIM, TILE), BF16),
            pltpu.VMEM((2, DIM, ROWS), BF16),
            pltpu.VMEM((2, DIM, ROWS), BF16),
            pltpu.VMEM((4, 2, ROWS, DIM), BF16),
            pltpu.VMEM((4, 2, ROWS, DIM), BF16),
            dma((8,)),
            dma((8, 2, 3)),
            dma((8, 2, 3)),
            dma((2, 3)),
            dma((2, 3)),
            dma((5,)),
            dma((5,)),
            dma((9,)),
            dma((9,)),
            dma((2,)),
            dma((2,)),
            dma((4, 2)),
            dma((4, 2)),
            pltpu.SemaphoreType.REGULAR((2,)),
        ],
        compiler_params=pltpu.CompilerParams(
            collective_id=0, has_side_effects=True, vmem_limit_bytes=24 * 1024 * 1024
        ),
    )(*[pltpu.with_memory_space_constraint(a, pltpu.HBM) for a in (query, key, value, out_saved, grad_out, log_norm, band, frames)])

    return tuple(grads[n * ROWS : (n + 1) * ROWS] for n in range(3))


def solution(mesh):
    rows = P(("slab", "space"), None)
    return jax.shard_map(
        functools.partial(body, mesh.shape["slab"], mesh.shape["space"]),
        mesh=mesh,
        in_specs=(rows, rows, rows, rows, rows, P(None, ("slab", "space")), P(), P()),
        out_specs=(rows, rows, rows),
        check_vma=False,
    )
```
